128 devices in a mesh: sx: 8 (over y, core), sy: 16 (over z, x).
Axes of the slice: x: 4, y: 4, z: 4, core: 2. Of those that a mesh axis runs over, the one named last changes fastest.
Arguments:
- features: bfloat16 [131072, 384], P(('sx', 'sy'))
- cotangent: bfloat16 [131072, 384], P(('sx', 'sy')), may hold values from -6 to 6
- hilbert_rank: int32 [131072], P(('sx', 'sy')), may hold values from 0 to 131071, as said below
- w_qkv: bfloat16 [384, 1152], replicated
- w_proj: bfloat16 [384, 384], replicated, may hold values from -0.3125 to 0.3125
Outputs:
- outputs: bfloat16 [131072, 384], P(('sx', 'sy'))
- grad_features: bfloat16 [131072, 384], P(('sx', 'sy'))
- grad_qkv: float32 [384, 1152], replicated
- grad_proj: float32 [384, 384], replicated
The draws below stay inside these ranges and needn't reach their ends.
Inputs may be any that keep to these rules, and one draw needn't show every extreme that they name: hilbert_rank is a permutation. Hilbert positions t * 1024 to (t + 1) * 1024 - 1 belong to device t. Every device sends rows to every device, 4 to 16 rows to each, and every device has 16 rows for some owners and receives 16 rows from some devices.
All inputs are finite; a program needn't handle non-finite values.
Results may differ from the reference program's by a relative error of at most 0.004.
The reference program's roundings to bfloat16 on the way count: a program that leaves them out, or rounds other values in their place, can miss the bound.
Values may be sent and summed in bfloat16 or wider, within the bound.
A program may use at most 64 MiB of HBM per device.

```python
import math
import jax
import jax.numpy as jnp
from jax import lax

C = 384
HEADS = 24
PATCH = 1024
ROWS = 1024
TOKENS = 131072


def draw_features(key, part):
    first_key = jax.random.fold_in(key, 0)
    values = jnp.clip(jax.random.normal(first_key, (TOKENS, C), jnp.float32), -6.0, 6.0)
    return values.astype(jnp.bfloat16)


def draw_w_qkv(key, part):
    first_key = jax.random.fold_in(key, 0)
    spread = (2.0 / C) ** 0.5
    base = jnp.clip(jax.random.normal(first_key, (C, 3 * C), jnp.float32), -6.0, 6.0) * spread
    values = base
    return values.astype(jnp.bfloat16)


def draw_hilbert_rank(key, part):
    devices = TOKENS // ROWS
    peer = ROWS // devices
    quarter = devices // 4
    count_table = jnp.concatenate([jnp.full((quarter,), 2 * peer, jnp.int32), jnp.full((quarter,), peer // 4 * 2, jnp.int32), jnp.full((devices - 2 * quarter,), 3 * peer // 4, jnp.int32)])
    count_table = jax.random.permutation(jax.random.fold_in(key, 11), count_table).astype(jnp.int32)
    ends = jnp.cumsum(count_table)
    slot_pos = jnp.arange(ROWS, dtype=jnp.int32)
    group = jnp.sum((slot_pos[:, None] >= ends[None, :]).astype(jnp.int32), axis=1)
    shuffle_src = jax.random.permutation(jax.random.fold_in(key, 12), devices).astype(jnp.int32)
    shuffle_dst = jax.random.permutation(jax.random.fold_in(key, 13), devices).astype(jnp.int32)
    target = shuffle_dst[(shuffle_src[:, None] + group[None, :]) % devices]

    def local_perm(sub_key):
        return jax.random.permutation(sub_key, ROWS).astype(jnp.int32)
    row_perm = jax.vmap(local_perm)(jax.random.split(jax.random.fold_in(key, 14), devices))
    pos_perm = jax.vmap(local_perm)(jax.random.split(jax.random.fold_in(key, 15), devices))
    position = pos_perm[target, slot_pos[None, :]]
    ranks = target * ROWS + position
    sources = jnp.arange(devices, dtype=jnp.int32)
    flat_index = sources[:, None] * ROWS + row_perm
    return jnp.zeros((devices * ROWS,), jnp.int32).at[flat_index.reshape(-1)].set(ranks.reshape(-1))


def steps_of(stream_key, extent, pieces, least, top_value):
    level, own = 1.0, jax.random.fold_in(stream_key, 6)
    for dim, parts in pieces:
        draws = jnp.exp(jax.random.uniform(jax.random.fold_in(own, dim), (parts,), jnp.float32, least / len(pieces), top_value / len(pieces)))
        level = level * jnp.repeat(draws, extent[dim] // parts).reshape([-1 if axis == dim else 1 for axis in range(len(extent))])
    return level


def gaussian(stream_key, shape, deviation, limit, cuts=(), held_as=jnp.bfloat16):
    entries = jax.random.normal(stream_key, shape, jnp.float32) * deviation
    if len(cuts) > 0:
        entries = steps_of(stream_key, shape, cuts, -0.22, 0.18) * entries
    return jnp.clip(entries, min=-limit, max=limit).astype(held_as)


def setup_inputs(seed: int = 0) -> dict:
    key_list = jax.random.split(jax.random.key(seed), 6)
    features = draw_features(jax.random.fold_in(key_list[5], 71), 0)
    cotangent = gaussian(key_list[1], (TOKENS, C), 1.0, 6.0, ((0, 128),))
    hilbert_rank = draw_hilbert_rank(jax.random.fold_in(key_list[5], 71), 0)
    w_qkv = draw_w_qkv(jax.random.fold_in(key_list[5], 71), 0)
    w_proj = gaussian(key_list[4], (C, C), C ** -0.5, 0.3125)
    return dict(features=features, cotangent=cotangent, hilbert_rank=hilbert_rank, w_qkv=w_qkv, w_proj=w_proj)


def contract(left_op, right_op, left_dim, right_dim):
    return lax.dot_general(left_op, right_op, (((left_dim,), (right_dim,)), ((), ())), preferred_element_type=jnp.float32)

def head_pass(query_rows, key_rows, value_rows, grad_slice):
    score_scale = query_rows.shape[1] ** (-0.5)
    scores = contract(query_rows, key_rows, 1, 1) * score_scale
    shifted = jnp.exp(scores - lax.optimization_barrier(jnp.max(scores, axis=1, keepdims=True)))
    prob_full = shifted / lax.optimization_barrier(jnp.sum(shifted, axis=1, keepdims=True))
    prob_low = prob_full.astype(jnp.bfloat16)
    attended = jnp.dot(prob_low, value_rows, preferred_element_type=jnp.float32).astype(jnp.bfloat16)
    dprobs = contract(grad_slice, value_rows, 1, 1)
    dscores = (prob_full * (dprobs - lax.optimization_barrier(jnp.sum(dprobs * prob_full, axis=1, keepdims=True))) * score_scale).astype(jnp.bfloat16)
    dquery = jnp.dot(dscores, key_rows, preferred_element_type=jnp.float32).astype(jnp.bfloat16)
    dkey_rows = contract(dscores, query_rows, 0, 0).astype(jnp.bfloat16)
    dvalue = contract(prob_low, grad_slice, 0, 0).astype(jnp.bfloat16)
    return (attended, dquery, dkey_rows, dvalue)

def patch_pass(block_rows, block_grads, w_qkv, w_proj, head_count):
    feat_width = block_rows.shape[1]
    head_dim = feat_width // head_count
    values = block_rows.astype(jnp.float32)
    row_mean = lax.optimization_barrier(jnp.mean(values, axis=1, keepdims=True))
    centred = values - row_mean
    inv_std = lax.rsqrt(lax.optimization_barrier(jnp.mean(centred * centred, axis=1, keepdims=True)) + 1e-05)
    normed = centred * inv_std
    normed_low = normed.astype(jnp.bfloat16)
    projected = jnp.dot(normed_low, w_qkv, preferred_element_type=jnp.float32).astype(jnp.bfloat16)
    upstream = contract(block_grads, w_proj, 1, 1).astype(jnp.bfloat16)

    def one_head(head_index):
        head_start = head_index * head_dim
        query_rows = lax.dynamic_slice_in_dim(projected, head_start, head_dim, 1)
        key_rows = lax.dynamic_slice_in_dim(projected, head_start + feat_width, head_dim, 1)
        value_rows = lax.dynamic_slice_in_dim(projected, head_start + 2 * feat_width, head_dim, 1)
        grad_slice = lax.dynamic_slice_in_dim(upstream, head_start, head_dim, 1)
        return head_pass(query_rows, key_rows, value_rows, grad_slice)
    heads_out = lax.map(one_head, jnp.arange(head_count, dtype=jnp.int32))

    def merge_heads(stacked):
        return jnp.transpose(stacked, (1, 0, 2)).reshape(stacked.shape[1], feat_width)
    attended = merge_heads(heads_out[0])
    dprojected = jnp.concatenate([merge_heads(heads_out[1]), merge_heads(heads_out[2]), merge_heads(heads_out[3])], axis=1)
    mixed_out = jnp.dot(attended, w_proj, preferred_element_type=jnp.float32)
    output = (values + mixed_out).astype(jnp.bfloat16)
    dnormed = contract(dprojected, w_qkv, 1, 1)
    dnorm_mean = lax.optimization_barrier(jnp.mean(dnormed, axis=1, keepdims=True))
    cross_mean = lax.optimization_barrier(jnp.mean(dnormed * normed, axis=1, keepdims=True))
    dinput = inv_std * (dnormed - dnorm_mean - normed * cross_mean)
    grad_input = (block_grads.astype(jnp.float32) + dinput).astype(jnp.bfloat16)
    return (output, grad_input, normed_low, dprojected, attended)

def reference(features, cotangent, hilbert_rank, w_qkv, w_proj):
    curve_rows = jnp.zeros_like(features).at[hilbert_rank].set(features)
    curve_grads = jnp.zeros_like(cotangent).at[hilbert_rank].set(cotangent)
    patch_total = TOKENS // PATCH

    def run_patch(both_blocks):
        return patch_pass(both_blocks[0], both_blocks[1], w_qkv, w_proj, HEADS)
    results = lax.map(run_patch, (curve_rows.reshape(patch_total, PATCH, C), curve_grads.reshape(patch_total, PATCH, C)))
    curve_out = results[0].reshape(TOKENS, C)
    curve_grad = results[1].reshape(TOKENS, C)
    normed_low = results[2].reshape(TOKENS, C)
    dprojected = results[3].reshape(TOKENS, 3 * C)
    attended = results[4].reshape(TOKENS, C)
    grad_scale = 1.0 / math.sqrt(TOKENS)
    grad_qkv = contract(normed_low, dprojected, 0, 0) * grad_scale
    grad_proj = contract(attended, curve_grads, 0, 0) * grad_scale
    return (curve_out[hilbert_rank], curve_grad[hilbert_rank], grad_qkv, grad_proj)
```

```python
import functools
import math

import jax
import jax.numpy as jnp
from jax import lax
from jax.experimental import pallas as pl
from jax.experimental.pallas import tpu as pltpu
from jax.sharding import PartitionSpec as P

BF = jnp.bfloat16
F32 = jnp.float32
HEADS = 24
ROWS = 1024
C = 384
DEV = 128
CAP = 16
SLOTS = DEV * CAP
EXT = 2 * C + 128
RC = 256
NR = ROWS // RC
SC = 256
VM = pl.BlockSpec(memory_space=pltpu.VMEM)
PARAMS = pltpu.CompilerParams(vmem_limit_bytes=60 * 1024 * 1024)


def dg(a, b, da, db):
    return lax.dot_general(a, b, (((da,), (db,)), ((), ())), preferred_element_type=F32)


def chunk(i, size):
    return pl.ds(pl.multiple_of(i * size, size), size)


def pack_kernel(x_ref, ct_ref, rank_ref, send_ref, slot_ref, rows):
    rank = jnp.concatenate([rank_ref[i : i + 1, :] for i in range(ROWS // 128)], axis=1)
    owner = rank // ROWS
    place = rank - owner * ROWS
    onehot = lax.broadcasted_iota(jnp.int32, (DEV, ROWS), 0) == owner
    before = (
        lax.broadcasted_iota(jnp.int32, (ROWS, ROWS), 0)
        < lax.broadcasted_iota(jnp.int32, (ROWS, ROWS), 1)
    )
    counts = jnp.dot(
        onehot.astype(F32).astype(BF), before.astype(F32).astype(BF), preferred_element_type=F32
    )
    earlier = jnp.sum(jnp.where(onehot, counts, 0.0), axis=0, keepdims=True)
    slot = owner * CAP + earlier.astype(jnp.int32)
    slot_ref[...] = jnp.broadcast_to(slot, slot_ref.shape)
    high = place // 32
    low = place - high * 32
    line = lax.broadcasted_iota(jnp.int32, (128, ROWS), 0)
    code = jnp.where(line == 0, high + 1, jnp.where(line == 1, low, 0)).astype(F32)
    rows[:, :C] = x_ref[...]
    rows[:, C : 2 * C] = ct_ref[...]
    rows[:, 2 * C :] = code.T.astype(BF)

    def step(i, _):
        pick = (lax.broadcasted_iota(jnp.int32, (SC, ROWS), 0) + i * SC) == slot
        send_ref[chunk(i, SC), :] = jnp.dot(
            pick.astype(F32).astype(BF), rows[...], preferred_element_type=F32
        ).astype(BF)
        return 0

    lax.fori_loop(0, SLOTS // SC, step, 0)


def last_kernel(ret_ref, slot_ref, out_ref, gx_ref, col):
    col[...] = jnp.broadcast_to(slot_ref[0:1, :].astype(F32), (128, ROWS)).T

    def step(i, _):
        rs = chunk(i, RC)
        ids = lax.broadcasted_iota(jnp.int32, (RC, SLOTS), 1).astype(F32)
        pick = (ids == col[rs, 0:1]).astype(F32).astype(BF)
        got = jnp.dot(pick, ret_ref[...], preferred_element_type=F32).astype(BF)
        out_ref[rs, :] = got[:, :C]
        gx_ref[rs, :] = got[:, C:]
        return 0

    lax.fori_loop(0, NR, step, 0)


def layer_norm(rows):
    v = rows.astype(F32)
    c = v - jnp.mean(v, axis=1, keepdims=True)
    inv = lax.rsqrt(jnp.mean(c * c, axis=1, keepdims=True) + 1e-5)
    return v, c * inv, inv


def patch_kernel(
    got_ref, wqkv_ref, wproj_ref, back_ref, gq_ref, gp_ref,
    rows, results, place_row, proj, up, proj_t, up_t, oacc, dqacc, dk_t, dv_t, low, dproj, att,
):
    def places(i, _):
        code = got_ref[chunk(i, SC), 2 * C :].astype(F32)
        t = code.T
        place_row[0:1, chunk(i, SC)] = (t[0:1, :] - 1.0) * 32.0 + t[1:2, :]
        return 0

    lax.fori_loop(0, SLOTS // SC, places, 0)

    def prologue(r, _):
        rs = chunk(r, RC)
        ids = (lax.broadcasted_iota(jnp.int32, (RC, SLOTS), 0) + r * RC).astype(F32)
        pick = (ids == place_row[0:1, :]).astype(F32).astype(BF)
        both = jnp.dot(pick, got_ref[:, : 2 * C], preferred_element_type=F32).astype(BF)
        rows[rs, :] = both
        _, n, _ = layer_norm(both[:, :C])
        nl = n.astype(BF)
        low[rs, :] = nl
        p = jnp.dot(nl, wqkv_ref[...], preferred_element_type=F32).astype(BF)
        u = dg(both[:, C:], wproj_ref[...], 1, 1).astype(BF)
        for g in range(9):
            blk = p[:, g * 128 : (g + 1) * 128]
            proj[g, rs, :] = blk
            if g < 3:
                proj_t[g * 128 : (g + 1) * 128, rs] = (blk * BF(0.25)).T
        for g in range(3):
            blk = u[:, g * 128 : (g + 1) * 128]
            up[g, rs, :] = blk
            up_t[g * 128 : (g + 1) * 128, rs] = blk.T
        return 0

    lax.fori_loop(0, NR, prologue, 0)
    oacc[...] = jnp.zeros_like(oacc)
    dqacc[...] = jnp.zeros_like(dqacc)
    lane = lax.broadcasted_iota(jnp.int32, (1, 128), 1) // 16

    def head(h, _):
        g = h // 8
        mask = (lane == (h - g * 8)).astype(F32).astype(BF)
        k = proj[3 + g]
        v = proj[6 + g]
        km = k * (mask * BF(0.25))
        vm = v * mask
        hs = chunk(h, 16)
        dk = jnp.zeros((16, ROWS), F32)
        dv = jnp.zeros((16, ROWS), F32)
        for r in range(NR):
            rs = slice(r * RC, (r + 1) * RC)
            qm = proj[g, rs, :] * (mask * BF(0.25))
            um = up[g, rs, :] * mask
            s = dg(qm, k, 1, 1)
            dp = dg(um, v, 1, 1)
            e = jnp.exp(s - jnp.max(s, axis=1, keepdims=True))
            linv = 1.0 / jnp.sum(e, axis=1, keepdims=True)
            mid = jnp.sum(e * dp, axis=1, keepdims=True) * linv
            p = e * linv
            pb = p.astype(BF)
            ds = (p * (dp - mid)).astype(BF)
            oacc[g, rs, :] += jnp.dot(pb, vm, preferred_element_type=F32)
            dqacc[g, rs, :] += jnp.dot(ds, km, preferred_element_type=F32)
            dk = dk + jnp.dot(proj_t[hs, rs], ds, preferred_element_type=F32)
            dv = dv + jnp.dot(up_t[hs, rs], pb, preferred_element_type=F32)
        dk_t[hs, :] = dk.astype(BF)
        dv_t[hs, :] = dv.astype(BF)
        return 0

    lax.fori_loop(0, HEADS, head, 0)
    gq_ref[...] = jnp.zeros_like(gq_ref)
    gp_ref[...] = jnp.zeros_like(gp_ref)

    def epilogue(r, _):
        rs = chunk(r, RC)
        v, n, inv = layer_norm(rows[rs, :C])
        for g in range(3):
            att[rs, g * 128 : (g + 1) * 128] = oacc[g, rs, :].astype(BF)
            dproj[rs, g * 128 : (g + 1) * 128] = dqacc[g, rs, :].astype(BF)
        dproj[rs, C : 2 * C] = dk_t[:, rs].T
        dproj[rs, 2 * C :] = dv_t[:, rs].T
        a = att[rs, :]
        dpj = dproj[rs, :]
        ct = rows[rs, C:]
        results[rs, :C] = (v + jnp.dot(a, wproj_ref[...], preferred_element_type=F32)).astype(BF)
        dn = dg(dpj, wqkv_ref[...], 1, 1)
        dm = jnp.mean(dn, axis=1, keepdims=True)
        cm = jnp.mean(dn * n, axis=1, keepdims=True)
        results[rs, C:] = (ct.astype(F32) + inv * (dn - dm - n * cm)).astype(BF)
        gq_ref[...] += dg(low[rs, :], dpj, 0, 0)
        gp_ref[...] += dg(a, ct, 0, 0)
        return 0

    lax.fori_loop(0, NR, epilogue, 0)

    def back(i, _):
        ss = chunk(i, SC)
        code = got_ref[ss, 2 * C :].astype(F32)
        place = (code[:, 0:1] - 1.0) * 32.0 + code[:, 1:2]
        ids = lax.broadcasted_iota(jnp.int32, (SC, ROWS), 1).astype(F32)
        pick = (ids == place).astype(F32).astype(BF)
        back_ref[ss, :] = jnp.dot(pick, results[...], preferred_element_type=F32).astype(BF)
        return 0

    lax.fori_loop(0, SLOTS // SC, back, 0)


def on_device(features, cotangent, hilbert_rank, w_qkv, w_proj):
    shape = jax.ShapeDtypeStruct
    send, slot = pl.pallas_call(
        pack_kernel,
        out_shape=(shape((SLOTS, EXT), BF), shape((8, ROWS), jnp.int32)),
        in_specs=[VM] * 3,
        out_specs=(VM,) * 2,
        scratch_shapes=[pltpu.VMEM((ROWS, EXT), BF)],
        compiler_params=PARAMS,
        name="pack",
    )(features, cotangent, hilbert_rank.reshape(ROWS // 128, 128))
    got = lax.all_to_all(
        send.reshape(DEV, CAP, EXT), ("sx", "sy"), split_axis=0, concat_axis=0, tiled=True
    ).reshape(SLOTS, EXT)
    back, grad_qkv, grad_proj = pl.pallas_call(
        patch_kernel,
        out_shape=(shape((SLOTS, 2 * C), BF), shape((C, 3 * C), F32), shape((C, C), F32)),
        in_specs=[VM] * 3,
        out_specs=(VM,) * 3,
        scratch_shapes=[
            pltpu.VMEM((ROWS, 2 * C), BF),
            pltpu.VMEM((ROWS, 2 * C), BF),
            pltpu.VMEM((8, SLOTS), F32),
            pltpu.VMEM((9, ROWS, 128), BF),
            pltpu.VMEM((3, ROWS, 128), BF),
            pltpu.VMEM((C, ROWS), BF),
            pltpu.VMEM((C, ROWS), BF),
            pltpu.VMEM((3, ROWS, 128), F32),
            pltpu.VMEM((3, ROWS, 128), F32),
            pltpu.VMEM((C, ROWS), BF),
            pltpu.VMEM((C, ROWS), BF),
            pltpu.VMEM((ROWS, C), BF),
            pltpu.VMEM((ROWS, 3 * C), BF),
            pltpu.VMEM((ROWS, C), BF),
        ],
        compiler_params=PARAMS,
        name="patch",
    )(got, w_qkv, w_proj)
    ret = lax.all_to_all(
        back.reshape(DEV, CAP, 2 * C), ("sx", "sy"), split_axis=0, concat_axis=0, tiled=True
    ).reshape(SLOTS, 2 * C)
    sums = lax.psum((grad_qkv, grad_proj), ("sx", "sy"))
    scale = 1.0 / math.sqrt(ROWS * DEV)
    outputs, grad_features = pl.pallas_call(
        last_kernel,
        out_shape=(shape((ROWS, C), BF), shape((ROWS, C), BF)),
        in_specs=[VM] * 2,
        out_specs=(VM,) * 2,
        scratch_shapes=[pltpu.VMEM((ROWS, 128), F32)],
        compiler_params=PARAMS,
        name="last",
    )(ret, slot)
    return outputs, grad_features, sums[0] * scale, sums[1] * scale


def solution(mesh):
    in_specs = (P(("sx", "sy"), None), P(("sx", "sy"), None), P(("sx", "sy")), P(), P())
    out_specs = (P(("sx", "sy"), None), P(("sx", "sy"), None), P(), P())
    return jax.shard_map(
        on_device, mesh=mesh, in_specs=in_specs, out_specs=out_specs, check_vma=False
    )
```

```python
import functools
import math

import jax
import jax.numpy as jnp
from jax import lax
from jax.experimental import pallas as pl
from jax.experimental.pallas import tpu as pltpu
from jax.sharding import PartitionSpec as P

BF = jnp.bfloat16
F32 = jnp.float32
MESH = pl.DeviceIdType.MESH
HEADS = 24
ROWS = 1024
C = 384
NX = 8
NY = 16
DEV = NX * NY
CHIPS = DEV // 2
CAP = 16
SLOTS = DEV * CAP
RC = 256
NR = ROWS // RC
SC = NY * CAP
FIRST = (0, 3072, 24)
SECOND = (3072, 2048, 16)
GROWS = FIRST[1] + SECOND[1]
VM = pl.BlockSpec(memory_space=pltpu.VMEM)
ANY = pl.BlockSpec(memory_space=pl.ANY)


def dg(a, b, da, db):
    return lax.dot_general(a, b, (((da,), (db,)), ((), ())), preferred_element_type=F32)


def chunk(i, size):
    return pl.ds(pl.multiple_of(i * size, size), size)


def hot(test):
    return test.astype(F32).astype(BF)


def iota(shape, dim):
    return lax.broadcasted_iota(jnp.int32, shape, dim).astype(F32)


def layer_norm(rows):
    v = rows.astype(F32)
    c = v - jnp.mean(v, axis=1, keepdims=True)
    inv = lax.rsqrt(jnp.mean(c * c, axis=1, keepdims=True) + 1e-5)
    return v, c * inv, inv


def wait_for(ref, sem):
    pltpu.make_async_copy(ref, ref, sem).wait()


class Reduction:
    def __init__(self, span, terms, total, half, own, part, mine, sem, sx, sy):
        self.base, self.count, self.piece = span
        self.terms, self.total = terms, total
        self.half, self.own, self.part, self.mine, self.sem = half, own, part, mine, sem
        self.core = lax.rem(sx, 2)
        self.chip = (sx // 2) * NY + sy
        self.partner = (sx + 1 - 2 * self.core, sy)

    def side(self, core):
        n = self.count // 2
        return pl.ds(pl.multiple_of(self.base + core * n, 8), n)

    def remote(self, src, dst, i, dev):
        return pltpu.make_async_remote_copy(
            src_ref=src, dst_ref=dst, send_sem=self.sem.at[i], recv_sem=self.sem.at[i + 1],
            device_id=dev, device_id_type=MESH,
        )

    def others(self, start):
        def go(d, _):
            t = lax.rem(self.chip + d, CHIPS)
            start(t, ((t // NY) * 2 + self.core, lax.rem(t, NY)))
            return 0

        lax.fori_loop(1, CHIPS, go, 0)

    def placed(self, t):
        n = self.count // 2
        return pl.ds(pl.multiple_of(self.base + self.core * n + t * self.piece, 8), self.piece)

    def pair(self):
        self.remote(self.terms.at[self.side(1 - self.core)], self.half, 0, self.partner).start()

    def scatter(self):
        wait_for(self.half, self.sem.at[1])
        self.own[...] = self.terms[self.side(self.core), :] + self.half[...]
        self.others(
            lambda t, dev: self.remote(
                self.own.at[chunk(t, self.piece)], self.part.at[chunk(self.chip, self.piece)], 2, dev
            ).start()
        )
        self.part[chunk(self.chip, self.piece), :] = self.own[chunk(self.chip, self.piece), :]

    def gather(self):
        rest = self.part.at[pl.ds(0, (CHIPS - 1) * self.piece)]
        wait_for(rest, self.sem.at[3])

        def add(t, acc):
            return acc + self.part[chunk(t, self.piece), :]

        self.mine[...] = lax.fori_loop(0, CHIPS, add, jnp.zeros((self.piece, 128), F32))
        pltpu.make_async_copy(
            self.mine, self.total.at[self.placed(self.chip)], self.sem.at[8]
        ).start()
        self.others(
            lambda t, dev: self.remote(
                self.mine, self.total.at[self.placed(self.chip)], 4, dev
            ).start()
        )

    def give(self):
        rest = self.part.at[pl.ds(0, (CHIPS - 1) * self.piece)]
        wait_for(rest, self.sem.at[5])
        wait_for(self.mine, self.sem.at[8])
        mine = self.total.at[self.side(self.core)]
        self.remote(mine, mine, 6, self.partner).start()

    def finish(self):
        rest = self.part.at[pl.ds(0, (CHIPS - 1) * self.piece)]
        wait_for(self.half, self.sem.at[7])
        wait_for(self.half, self.sem.at[6])
        wait_for(rest, self.sem.at[4])
        wait_for(rest, self.sem.at[2])
        wait_for(self.half, self.sem.at[0])


def patch_kernel(
    x_ref, ct_ref, rank_ref, wqkv_ref, wproj_ref,
    ret_ref, total_ref, slot_ref,
    send, got, back, place_out, place_in, place_row, pick, rows, results,
    proj, up, proj_t, up_t, oacc, dqacc, dk_t, dv_t, low_t, ct_t, dproj, att, terms,
    half_a, own_a, part_a, mine_a, half_b, own_b, part_b, mine_b, sem_a, sem_b, sem,
):
    sx = lax.axis_index("sx")
    sy = lax.axis_index("sy")
    me = sx * NY + sy
    barrier = pltpu.get_barrier_semaphore()

    def greet(d, _):
        t = lax.rem(me + d, DEV)
        pl.semaphore_signal(barrier, 1, device_id=(t // NY, lax.rem(t, NY)), device_id_type=MESH)
        return 0

    lax.fori_loop(1, DEV, greet, 0)
    sums = (
        Reduction(FIRST, terms, total_ref, half_a, own_a, part_a, mine_a, sem_a, sx, sy),
        Reduction(SECOND, terms, total_ref, half_b, own_b, part_b, mine_b, sem_b, sx, sy),
    )

    def copy_to(src, dst, t, i):
        pltpu.make_async_remote_copy(
            src_ref=src, dst_ref=dst, send_sem=sem.at[i], recv_sem=sem.at[i + 1],
            device_id=(t // NY, lax.rem(t, NY)), device_id_type=MESH,
        ).start()

    def send_part(part, ref, dst, step, i):
        tx = lax.rem(sx + step, NX)

        def go(d, _):
            t = tx * NY + lax.rem(sy + d, NY)
            copy_to(ref.at[part, chunk(t, CAP)], dst.at[part, chunk(me, CAP)], t, i)
            return 0

        lax.fori_loop(jnp.where(step == 0, 1, 0), NY, go, 0)

    rank = jnp.concatenate([rank_ref[i : i + 1, :] for i in range(ROWS // 128)], axis=1)
    owner = rank // ROWS
    place = rank - owner * ROWS
    owned = iota((DEV, ROWS), 0) == owner.astype(F32)
    before = iota((ROWS, ROWS), 0) < iota((ROWS, ROWS), 1)
    counts = jnp.dot(hot(owned), hot(before), preferred_element_type=F32)
    earlier = jnp.sum(jnp.where(owned, counts, 0.0), axis=0, keepdims=True)
    slot = owner.astype(F32) * CAP + earlier
    slot_ref[...] = jnp.broadcast_to(slot, slot_ref.shape)
    high = place // 32
    line = iota((128, ROWS), 0) == earlier
    codes = [
        dg(hot(owned), jnp.where(line, v.astype(F32), 0.0).astype(BF), 1, 1)
        for v in (high + 1, place - high * 32)
    ]
    place_out[...] = (codes[0] * 32.0 + codes[1]).reshape(DEV, 1, 128)
    pl.semaphore_wait(barrier, DEV - 1)

    def packs(part, src):
        def step(k, _):
            tx = lax.rem(sx + k, NX)
            ids = iota((SC, ROWS), 0) + (tx * SC).astype(F32)
            send[part, chunk(tx, SC), :] = jnp.dot(
                hot(ids == slot), src[...], preferred_element_type=F32
            ).astype(BF)

            @pl.when(k > 0)
            def _():
                send_part(part, send, got, k - 1, 2 * part)

            return 0

        lax.fori_loop(0, NX, step, 0)

    packs(0, x_ref)

    def send_place(d, _):
        t = lax.rem(me + d, DEV)
        copy_to(place_out.at[t], place_in.at[me], t, 4)
        return 0

    lax.fori_loop(1, DEV, send_place, 0)
    place_in[me] = place_out[me]
    send_part(0, send, got, NX - 1, 0)
    packs(1, ct_ref)
    send_part(1, send, got, NX - 1, 2)
    mine = chunk(me, CAP)
    got[0, mine, :] = send[0, mine, :]
    got[1, mine, :] = send[1, mine, :]

    wait_for(place_in.at[pl.ds(0, DEV - 1)], sem.at[5])
    code = place_in[...].reshape(DEV, 128).T[0:CAP, :]
    big = jnp.floor(code * (1.0 / 32.0))
    spread = hot(iota((DEV, SLOTS), 0) == jnp.floor(iota((DEV, SLOTS), 1) * (1.0 / CAP)))
    both = [
        jnp.dot(v.astype(BF), spread, preferred_element_type=F32)
        for v in (big, code - big * 32.0)
    ]
    lanes = iota((CAP, SLOTS), 1)
    keep = (lanes - jnp.floor(lanes * (1.0 / CAP)) * CAP) == iota((CAP, SLOTS), 0)
    found = jnp.sum(jnp.where(keep, both[0] * 32.0 + both[1], 0.0), axis=0, keepdims=True)
    place_row[...] = jnp.broadcast_to(found - 32.0, place_row.shape)

    wait_for(got.at[0, pl.ds(0, SLOTS - CAP)], sem.at[1])

    def forward_rows(r, _):
        rs = chunk(r, RC)
        ids = iota((RC, SLOTS), 0) + (r * RC).astype(F32)
        q = hot(ids == place_row[0:1, :])
        pick[rs, :] = q
        x = jnp.dot(q, got[0], preferred_element_type=F32).astype(BF)
        rows[rs, :C] = x
        _, n, _ = layer_norm(x)
        nl = n.astype(BF)
        low_t[:, rs] = nl.T
        p = jnp.dot(nl, wqkv_ref[...], preferred_element_type=F32).astype(BF)
        for g in range(9):
            blk = p[:, g * 128 : (g + 1) * 128]
            proj[g, rs, :] = blk
            if g < 3:
                proj_t[g * 128 : (g + 1) * 128, rs] = (blk * BF(0.25)).T
        return 0

    lax.fori_loop(0, NR, forward_rows, 0)
    oacc[...] = jnp.zeros_like(oacc)
    dqacc[...] = jnp.zeros_like(dqacc)
    terms[GROWS - SECOND[1] + 4 * C :, :] = jnp.zeros((SECOND[1] - 4 * C, 128), F32)
    wait_for(got.at[1, pl.ds(0, SLOTS - CAP)], sem.at[3])

    def upstream_rows(r, _):
        rs = chunk(r, RC)
        ct = jnp.dot(pick[rs, :], got[1], preferred_element_type=F32).astype(BF)
        rows[rs, C:] = ct
        ct_t[:, rs] = ct.T
        u = dg(ct, wproj_ref[...], 1, 1).astype(BF)
        for g in range(3):
            blk = u[:, g * 128 : (g + 1) * 128]
            up[g, rs, :] = blk
            up_t[g * 128 : (g + 1) * 128, rs] = blk.T
        return 0

    lax.fori_loop(0, NR, upstream_rows, 0)
    lane = lax.broadcasted_iota(jnp.int32, (1, 128), 1) // 16

    def head(h, _):
        g = h // 8
        mask = hot(lane == (h - g * 8))
        k = proj[3 + g]
        v = proj[6 + g]
        km = k * (mask * BF(0.25))
        vm = v * mask
        hs = chunk(h, 16)
        dk = jnp.zeros((16, ROWS), F32)
        dv = jnp.zeros((16, ROWS), F32)
        for r in range(NR):
            rs = slice(r * RC, (r + 1) * RC)
            qm = proj[g, rs, :] * (mask * BF(0.25))
            um = up[g, rs, :] * mask
            s = dg(qm, k, 1, 1)
            dp = dg(um, v, 1, 1)
            e = jnp.exp(s - jnp.max(s, axis=1, keepdims=True))
            linv = 1.0 / jnp.sum(e, axis=1, keepdims=True)
            mid = jnp.sum(e * dp, axis=1, keepdims=True) * linv
            p = e * linv
            pb = p.astype(BF)
            ds = (p * (dp - mid)).astype(BF)
            oacc[g, rs, :] += jnp.dot(pb, vm, preferred_element_type=F32)
            dqacc[g, rs, :] += jnp.dot(ds, km, preferred_element_type=F32)
            dk = dk + jnp.dot(proj_t[hs, rs], ds, preferred_element_type=F32)
            dv = dv + jnp.dot(up_t[hs, rs], pb, preferred_element_type=F32)
        dk_t[hs, :] = dk.astype(BF)
        dv_t[hs, :] = dv.astype(BF)

        @pl.when(h == 17)
        def _():
            sums[0].scatter()

        @pl.when(h == 20)
        def _():
            sums[0].gather()

        @pl.when(h == 23)
        def _():
            sums[0].give()

        @pl.when(h - g * 8 == 7)
        def _():
            gs = chunk(g, 128)
            base = g * (4 * C)
            parts = (
                dqacc[g].astype(BF),
                dk_t[gs, :].T,
                dv_t[gs, :].T,
                oacc[g].astype(BF),
            )
            for i, part in enumerate(parts):
                if i < 3:
                    dproj[i, g] = part
                else:
                    att[g] = part
                terms[pl.ds(pl.multiple_of(base + i * C, 128), C), :] = jnp.dot(
                    (ct_t if i == 3 else low_t)[...], part, preferred_element_type=F32
                )

        @pl.when(h == 15)
        def _():
            sums[0].pair()

        return 0

    lax.fori_loop(0, HEADS, head, 0)
    sums[1].pair()

    def epilogue(r, _):
        rs = chunk(r, RC)
        v, n, inv = layer_norm(rows[rs, :C])
        a = jnp.concatenate([att[g, rs, :] for g in range(3)], axis=1)
        dpj = jnp.concatenate([dproj[i, g, rs, :] for i in range(3) for g in range(3)], axis=1)
        ct = rows[rs, C:]
        results[rs, :C] = (v + jnp.dot(a, wproj_ref[...], preferred_element_type=F32)).astype(BF)
        dn = dg(dpj, wqkv_ref[...], 1, 1)
        dm = jnp.mean(dn, axis=1, keepdims=True)
        cm = jnp.mean(dn * n, axis=1, keepdims=True)
        results[rs, C:] = (ct.astype(F32) + inv * (dn - dm - n * cm)).astype(BF)
        return 0

    lax.fori_loop(0, NR, epilogue, 0)
    sums[1].scatter()

    def send_back(step):
        tx = lax.rem(sx + step, NX)

        def go(d, _):
            t = tx * NY + lax.rem(sy + d, NY)
            copy_to(back.at[chunk(t, CAP)], ret_ref.at[chunk(me, CAP)], t, 6)
            return 0

        lax.fori_loop(jnp.where(step == 0, 1, 0), NY, go, 0)

    def backs(k, _):
        tx = lax.rem(sx + k, NX)
        ss = chunk(tx, SC)
        spot = jnp.broadcast_to(place_row[0:1, ss], (128, SC)).T[:, 0:1]
        q = hot(iota((SC, ROWS), 1) == spot)
        back[ss, :] = jnp.dot(q, results[...], preferred_element_type=F32).astype(BF)

        @pl.when(k > 0)
        def _():
            send_back(k - 1)

        return 0

    lax.fori_loop(0, NX // 2, backs, 0)
    sums[1].gather()
    lax.fori_loop(NX // 2, NX, backs, 0)
    send_back(NX - 1)
    own = pltpu.make_async_copy(back.at[mine], ret_ref.at[mine], sem.at[8])
    own.start()
    sums[1].give()
    for part in range(2):
        wait_for(send.at[part, pl.ds(0, SLOTS - CAP)], sem.at[2 * part])
    wait_for(place_out.at[pl.ds(0, DEV - 1)], sem.at[4])
    own.wait()
    for i in range(6, 8):
        wait_for(back.at[pl.ds(0, SLOTS - CAP)], sem.at[i])
    sums[0].finish()
    sums[1].finish()


def last_kernel(scale, ret_ref, slot_ref, total_ref, out_ref, gx_ref, gq_ref, gp_ref, col):
    col[...] = jnp.broadcast_to(slot_ref[0:1, :], (128, ROWS)).T

    def step(i, _):
        rs = chunk(i, RC)
        q = hot(iota((RC, SLOTS), 1) == col[rs, 0:1])
        row = jnp.dot(q, ret_ref[...], preferred_element_type=F32).astype(BF)
        out_ref[rs, :] = row[:, :C]
        gx_ref[rs, :] = row[:, C:]
        return 0

    lax.fori_loop(0, NR, step, 0)
    for g in range(3):
        for i in range(4):
            block = total_ref[(4 * g + i) * C : (4 * g + i + 1) * C, :] * scale
            if i < 3:
                gq_ref[:, i * C + g * 128 : i * C + (g + 1) * 128] = block
            else:
                gp_ref[g * 128 : (g + 1) * 128, :] = block.T


def on_device(features, cotangent, hilbert_rank, w_qkv, w_proj):
    shape = jax.ShapeDtypeStruct
    vm = pltpu.VMEM
    dma = pltpu.SemaphoreType.DMA

    def room(span):
        return [
            vm((span[1] // 2, 128), F32), vm((span[1] // 2, 128), F32),
            vm((span[1] // 2, 128), F32), vm((span[2], 128), F32),
        ]

    ret, total, slot = pl.pallas_call(
        patch_kernel,
        out_shape=(shape((SLOTS, 2 * C), BF), shape((GROWS, 128), F32), shape((8, ROWS), F32)),
        in_specs=[VM] * 5,
        out_specs=(ANY, ANY, VM),
        scratch_shapes=[
            vm((2, SLOTS, C), BF), vm((2, SLOTS, C), BF), vm((SLOTS, 2 * C), BF),
            vm((DEV, 1, 128), F32), vm((DEV, 1, 128), F32), vm((8, SLOTS), F32),
            vm((ROWS, SLOTS), BF), vm((ROWS, 2 * C), BF), vm((ROWS, 2 * C), BF),
            vm((9, ROWS, 128), BF), vm((3, ROWS, 128), BF), vm((C, ROWS), BF), vm((C, ROWS), BF),
            vm((3, ROWS, 128), F32), vm((3, ROWS, 128), F32), vm((C, ROWS), BF), vm((C, ROWS), BF),
            vm((C, ROWS), BF), vm((C, ROWS), BF), vm((3, 3, ROWS, 128), BF), vm((3, ROWS, 128), BF),
            vm((GROWS, 128), F32),
        ] + room(FIRST) + room(SECOND) + [dma((9,)), dma((9,)), dma((9,))],
        compiler_params=pltpu.CompilerParams(
            vmem_limit_bytes=62 * 1024 * 1024, collective_id=0, has_side_effects=True
        ),
        name="patch",
    )(features, cotangent, hilbert_rank.reshape(ROWS // 128, 128), w_qkv, w_proj)
    return pl.pallas_call(
        functools.partial(last_kernel, 1.0 / math.sqrt(ROWS * DEV)),
        out_shape=(
            shape((ROWS, C), BF), shape((ROWS, C), BF), shape((C, 3 * C), F32), shape((C, C), F32),
        ),
        in_specs=[VM] * 3,
        out_specs=(VM,) * 4,
        scratch_shapes=[vm((ROWS, 128), F32)],
        compiler_params=pltpu.CompilerParams(vmem_limit_bytes=60 * 1024 * 1024),
        name="last",
    )(ret, slot, total)


def solution(mesh):
    in_specs = (P(("sx", "sy"), None), P(("sx", "sy"), None), P(("sx", "sy")), P(), P())
    out_specs = (P(("sx", "sy"), None), P(("sx", "sy"), None), P(), P())
    return jax.shard_map(
        on_device, mesh=mesh, in_specs=in_specs, out_specs=out_specs, check_vma=False
    )
```

```python
import functools
import math

import jax
import jax.numpy as jnp
from jax import lax
from jax.experimental import pallas as pl
from jax.experimental.pallas import tpu as pltpu
from jax.sharding import PartitionSpec as P

BF = jnp.bfloat16
F32 = jnp.float32
MESH = pl.DeviceIdType.MESH
HEADS = 24
ROWS = 1024
C = 384
NX = 8
NY = 16
DEV = NX * NY
CHIPS = DEV // 2
CAP = 16
SLOTS = DEV * CAP
RC = 256
HC = 512
NR = ROWS // RC
SC = NY * CAP
FIRST = (0, 3072, 24)
SECOND = (3072, 2048, 16)
GROWS = FIRST[1] + SECOND[1]
VM = pl.BlockSpec(memory_space=pltpu.VMEM)
ANY = pl.BlockSpec(memory_space=pl.ANY)


def dg(a, b, da, db):
    return lax.dot_general(a, b, (((da,), (db,)), ((), ())), preferred_element_type=F32)


def chunk(i, size):
    return pl.ds(pl.multiple_of(i * size, size), size)


def hot(test):
    return test.astype(F32).astype(BF)


def iota(shape, dim):
    return lax.broadcasted_iota(jnp.int32, shape, dim).astype(F32)


def layer_norm(rows):
    v = rows.astype(F32)
    c = v - jnp.mean(v, axis=1, keepdims=True)
    inv = lax.rsqrt(jnp.mean(c * c, axis=1, keepdims=True) + 1e-5)
    return v, c * inv, inv


def wait_for(ref, sem):
    pltpu.make_async_copy(ref, ref, sem).wait()


class Reduction:
    def __init__(self, span, terms, total, half, own, part, mine, sem, sx, sy):
        self.base, self.count, self.piece = span
        self.terms, self.total = terms, total
        self.half, self.own, self.part, self.mine, self.sem = half, own, part, mine, sem
        self.core = lax.rem(sx, 2)
        self.chip = (sx // 2) * NY + sy
        self.partner = (sx + 1 - 2 * self.core, sy)

    def side(self, core):
        n = self.count // 2
        return pl.ds(pl.multiple_of(self.base + core * n, 8), n)

    def remote(self, src, dst, i, dev):
        return pltpu.make_async_remote_copy(
            src_ref=src, dst_ref=dst, send_sem=self.sem.at[i], recv_sem=self.sem.at[i + 1],
            device_id=dev, device_id_type=MESH,
        )

    def others(self, start):
        def go(d, _):
            t = lax.rem(self.chip + d, CHIPS)
            start(t, ((t // NY) * 2 + self.core, lax.rem(t, NY)))
            return 0

        lax.fori_loop(1, CHIPS, go, 0)

    def placed(self, t):
        n = self.count // 2
        return pl.ds(pl.multiple_of(self.base + self.core * n + t * self.piece, 8), self.piece)

    def pair(self):
        self.remote(self.terms.at[self.side(1 - self.core)], self.half, 0, self.partner).start()

    def scatter(self):
        wait_for(self.half, self.sem.at[1])
        self.own[...] = self.terms[self.side(self.core), :] + self.half[...]
        self.others(
            lambda t, dev: self.remote(
                self.own.at[chunk(t, self.piece)], self.part.at[chunk(self.chip, self.piece)], 2, dev
            ).start()
        )
        self.part[chunk(self.chip, self.piece), :] = self.own[chunk(self.chip, self.piece), :]

    def gather(self):
        rest = self.part.at[pl.ds(0, (CHIPS - 1) * self.piece)]
        wait_for(rest, self.sem.at[3])

        def add(t, acc):
            return acc + self.part[chunk(t, self.piece), :]

        self.mine[...] = lax.fori_loop(0, CHIPS, add, jnp.zeros((self.piece, 128), F32))
        pltpu.make_async_copy(
            self.mine, self.total.at[self.placed(self.chip)], self.sem.at[8]
        ).start()
        self.others(
            lambda t, dev: self.remote(
                self.mine, self.total.at[self.placed(self.chip)], 4, dev
            ).start()
        )

    def give(self):
        rest = self.part.at[pl.ds(0, (CHIPS - 1) * self.piece)]
        wait_for(rest, self.sem.at[5])
        wait_for(self.mine, self.sem.at[8])
        mine = self.total.at[self.side(self.core)]
        self.remote(mine, mine, 6, self.partner).start()

    def finish(self):
        rest = self.part.at[pl.ds(0, (CHIPS - 1) * self.piece)]
        wait_for(self.half, self.sem.at[7])
        wait_for(self.half, self.sem.at[6])
        wait_for(rest, self.sem.at[4])
        wait_for(rest, self.sem.at[2])
        wait_for(self.half, self.sem.at[0])


def patch_kernel(
    x_ref, ct_ref, rank_ref, wqkv_ref, wproj_ref,
    out_ref, gx_ref, total_ref,
    send, got, ret, slot_row, place_out, place_in, place_row, pick, rows, results,
    proj, up, proj_t, up_t, oacc, dqacc, dk_t, dv_t, low_t, ct_t, dproj, att, terms,
    half_a, own_a, part_a, mine_a, half_b, own_b, part_b, mine_b, sem_a, sem_b, sem,
):
    sx = lax.axis_index("sx")
    sy = lax.axis_index("sy")
    me = sx * NY + sy
    barrier = pltpu.get_barrier_semaphore()

    def greet(d, _):
        t = lax.rem(me + d, DEV)
        pl.semaphore_signal(barrier, 1, device_id=(t // NY, lax.rem(t, NY)), device_id_type=MESH)
        return 0

    lax.fori_loop(1, DEV, greet, 0)
    sums = (
        Reduction(FIRST, terms, total_ref, half_a, own_a, part_a, mine_a, sem_a, sx, sy),
        Reduction(SECOND, terms, total_ref, half_b, own_b, part_b, mine_b, sem_b, sx, sy),
    )

    def copy_to(src, dst, t, i):
        pltpu.make_async_remote_copy(
            src_ref=src, dst_ref=dst, send_sem=sem.at[i], recv_sem=sem.at[i + 1],
            device_id=(t // NY, lax.rem(t, NY)), device_id_type=MESH,
        ).start()

    def send_part(part, ref, dst, step, i):
        tx = lax.rem(sx + step, NX)

        def go(d, _):
            t = tx * NY + lax.rem(sy + d, NY)
            copy_to(ref.at[part, chunk(t, CAP)], dst.at[part, chunk(me, CAP)], t, i)
            return 0

        lax.fori_loop(jnp.where(step == 0, 1, 0), NY, go, 0)

    rank = jnp.concatenate([rank_ref[i : i + 1, :] for i in range(ROWS // 128)], axis=1)
    owner = rank // ROWS
    place = rank - owner * ROWS
    owned = iota((DEV, ROWS), 0) == owner.astype(F32)
    before = iota((ROWS, ROWS), 0) < iota((ROWS, ROWS), 1)
    counts = jnp.dot(hot(owned), hot(before), preferred_element_type=F32)
    earlier = jnp.sum(jnp.where(owned, counts, 0.0), axis=0, keepdims=True)
    slot = owner.astype(F32) * CAP + earlier
    slot_row[...] = jnp.broadcast_to(slot, slot_row.shape)
    high = place // 32
    line = iota((128, ROWS), 0) == earlier
    codes = [
        dg(hot(owned), jnp.where(line, v.astype(F32), 0.0).astype(BF), 1, 1)
        for v in (high + 1, place - high * 32)
    ]
    place_out[...] = (codes[0] * 32.0 + codes[1]).reshape(DEV, 1, 128)
    pl.semaphore_wait(barrier, DEV - 1)

    def packs(part, src):
        def step(k, _):
            tx = lax.rem(sx + k, NX)
            ids = iota((SC, ROWS), 0) + (tx * SC).astype(F32)
            send[part, chunk(tx, SC), :] = jnp.dot(
                hot(ids == slot), src[...], preferred_element_type=F32
            ).astype(BF)

            @pl.when(k > 0)
            def _():
                send_part(part, send, got, k - 1, 2 * part)

            return 0

        lax.fori_loop(0, NX, step, 0)

    packs(0, x_ref)

    def send_place(d, _):
        t = lax.rem(me + d, DEV)
        copy_to(place_out.at[t], place_in.at[me], t, 4)
        return 0

    lax.fori_loop(1, DEV, send_place, 0)
    place_in[me] = place_out[me]
    send_part(0, send, got, NX - 1, 0)
    packs(1, ct_ref)
    send_part(1, send, got, NX - 1, 2)
    mine = chunk(me, CAP)
    got[0, mine, :] = send[0, mine, :]
    got[1, mine, :] = send[1, mine, :]

    wait_for(place_in.at[pl.ds(0, DEV - 1)], sem.at[5])
    code = place_in[...].reshape(DEV, 128).T[0:CAP, :]
    big = jnp.floor(code * (1.0 / 32.0))
    spread = hot(iota((DEV, SLOTS), 0) == jnp.floor(iota((DEV, SLOTS), 1) * (1.0 / CAP)))
    both = [
        jnp.dot(v.astype(BF), spread, preferred_element_type=F32)
        for v in (big, code - big * 32.0)
    ]
    lanes = iota((CAP, SLOTS), 1)
    keep = (lanes - jnp.floor(lanes * (1.0 / CAP)) * CAP) == iota((CAP, SLOTS), 0)
    found = jnp.sum(jnp.where(keep, both[0] * 32.0 + both[1], 0.0), axis=0, keepdims=True)
    place_row[...] = jnp.broadcast_to(found - 32.0, place_row.shape)

    wait_for(got.at[0, pl.ds(0, SLOTS - CAP)], sem.at[1])

    def forward_rows(r, _):
        rs = chunk(r, RC)
        ids = iota((RC, SLOTS), 0) + (r * RC).astype(F32)
        q = hot(ids == place_row[0:1, :])
        pick[rs, :] = q
        x = jnp.dot(q, got[0], preferred_element_type=F32).astype(BF)
        rows[rs, :C] = x
        _, n, _ = layer_norm(x)
        nl = n.astype(BF)
        low_t[:, rs] = nl.T
        p = jnp.dot(nl, wqkv_ref[...], preferred_element_type=F32).astype(BF)
        for g in range(9):
            blk = p[:, g * 128 : (g + 1) * 128]
            proj[g, rs, :] = blk
            if g < 3:
                proj_t[g * 128 : (g + 1) * 128, rs] = (blk * BF(0.25)).T
        return 0

    lax.fori_loop(0, NR, forward_rows, 0)
    oacc[...] = jnp.zeros_like(oacc)
    dqacc[...] = jnp.zeros_like(dqacc)
    terms[GROWS - SECOND[1] + 4 * C :, :] = jnp.zeros((SECOND[1] - 4 * C, 128), F32)
    wait_for(got.at[1, pl.ds(0, SLOTS - CAP)], sem.at[3])

    def upstream_rows(r, _):
        rs = chunk(r, RC)
        ct = jnp.dot(pick[rs, :], got[1], preferred_element_type=F32).astype(BF)
        rows[rs, C:] = ct
        ct_t[:, rs] = ct.T
        u = dg(ct, wproj_ref[...], 1, 1).astype(BF)
        for g in range(3):
            blk = u[:, g * 128 : (g + 1) * 128]
            up[g, rs, :] = blk
            up_t[g * 128 : (g + 1) * 128, rs] = blk.T
        return 0

    lax.fori_loop(0, NR, upstream_rows, 0)
    lane = lax.broadcasted_iota(jnp.int32, (1, 128), 1) // 16

    def head(h, _):
        g = h // 8
        mask = hot(lane == (h - g * 8))
        k = proj[3 + g]
        v = proj[6 + g]
        km = k * (mask * BF(0.25))
        vm = v * mask
        hs = chunk(h, 16)
        dk = jnp.zeros((16, ROWS), F32)
        dv = jnp.zeros((16, ROWS), F32)
        for r in range(ROWS // HC):
            rs = slice(r * HC, (r + 1) * HC)
            qm = proj[g, rs, :] * (mask * BF(0.25))
            um = up[g, rs, :] * mask
            s = dg(qm, k, 1, 1)
            dp = dg(um, v, 1, 1)
            e = jnp.exp(s - jnp.max(s, axis=1, keepdims=True))
            linv = 1.0 / jnp.sum(e, axis=1, keepdims=True)
            mid = jnp.sum(e * dp, axis=1, keepdims=True) * linv
            p = e * linv
            pb = p.astype(BF)
            ds = (p * (dp - mid)).astype(BF)
            oacc[g, rs, :] += jnp.dot(pb, vm, preferred_element_type=F32)
            dqacc[g, rs, :] += jnp.dot(ds, km, preferred_element_type=F32)
            dk = dk + jnp.dot(proj_t[hs, rs], ds, preferred_element_type=F32)
            dv = dv + jnp.dot(up_t[hs, rs], pb, preferred_element_type=F32)
        dk_t[hs, :] = dk.astype(BF)
        dv_t[hs, :] = dv.astype(BF)

        @pl.when(h == 16)
        def _():
            sums[0].scatter()

        @pl.when(h == 21)
        def _():
            sums[0].gather()

        @pl.when(h - g * 8 == 7)
        def _():
            gs = chunk(g, 128)
            base = g * (4 * C)
            parts = (
                dqacc[g].astype(BF),
                dk_t[gs, :].T,
                dv_t[gs, :].T,
                oacc[g].astype(BF),
            )
            for i, part in enumerate(parts):
                if i < 3:
                    dproj[i, g] = part
                else:
                    att[g] = part
                terms[pl.ds(pl.multiple_of(base + i * C, 128), C), :] = jnp.dot(
                    (ct_t if i == 3 else low_t)[...], part, preferred_element_type=F32
                )

        @pl.when(h == 15)
        def _():
            sums[0].pair()

        return 0

    lax.fori_loop(0, HEADS, head, 0)
    sums[1].pair()

    def epilogue(r, _):
        @pl.when(r == 1)
        def _():
            sums[1].scatter()

        rs = chunk(r, RC)
        v, n, inv = layer_norm(rows[rs, :C])
        a = jnp.concatenate([att[g, rs, :] for g in range(3)], axis=1)
        dpj = jnp.concatenate([dproj[i, g, rs, :] for i in range(3) for g in range(3)], axis=1)
        ct = rows[rs, C:]
        results[rs, :C] = (v + jnp.dot(a, wproj_ref[...], preferred_element_type=F32)).astype(BF)
        dn = dg(dpj, wqkv_ref[...], 1, 1)
        dm = jnp.mean(dn, axis=1, keepdims=True)
        cm = jnp.mean(dn * n, axis=1, keepdims=True)
        results[rs, C:] = (ct.astype(F32) + inv * (dn - dm - n * cm)).astype(BF)
        return 0

    lax.fori_loop(0, NR, epilogue, 0)
    sums[0].give()
    sums[1].gather()
    for part in range(2):
        wait_for(send.at[part, pl.ds(0, SLOTS - CAP)], sem.at[2 * part])

    def backs(part):
        def step(k, _):
            tx = lax.rem(sx + k, NX)
            ss = chunk(tx, SC)
            spot = jnp.broadcast_to(place_row[0:1, ss], (128, SC)).T[:, 0:1]
            q = hot(iota((SC, ROWS), 1) == spot)
            send[part, ss, :] = jnp.dot(
                q, results[:, part * C : (part + 1) * C], preferred_element_type=F32
            ).astype(BF)

            @pl.when(k > 0)
            def _():
                send_part(part, send, ret, k - 1, 6 + 2 * part)

            return 0

        lax.fori_loop(0, NX, step, 0)
        send_part(part, send, ret, NX - 1, 6 + 2 * part)
        ret[part, mine, :] = send[part, mine, :]

    backs(0)
    backs(1)

    def takes(r, _):
        rs = chunk(r, RC)
        spot = jnp.broadcast_to(slot_row[0:1, rs], (128, RC)).T[:, 0:1]
        pick[rs, :] = hot(iota((RC, SLOTS), 1) == spot)
        return 0

    lax.fori_loop(0, NR, takes, 0)
    sums[1].give()
    for part, dst in enumerate((out_ref, gx_ref)):
        wait_for(ret.at[part, pl.ds(0, SLOTS - CAP)], sem.at[7 + 2 * part])

        def unpack(r, _, part=part, dst=dst):
            rs = chunk(r, RC)
            dst[rs, :] = jnp.dot(pick[rs, :], ret[part], preferred_element_type=F32).astype(BF)
            return 0

        lax.fori_loop(0, NR, unpack, 0)
    wait_for(place_out.at[pl.ds(0, DEV - 1)], sem.at[4])
    for part in range(2):
        wait_for(send.at[part, pl.ds(0, SLOTS - CAP)], sem.at[6 + 2 * part])
    sums[0].finish()
    sums[1].finish()


def last_kernel(scale, x_ref, g_ref, total_ref, out_ref, gx_ref, gq_ref, gp_ref):
    out_ref[...] = x_ref[...]
    gx_ref[...] = g_ref[...]
    for g in range(3):
        for i in range(4):
            block = total_ref[(4 * g + i) * C : (4 * g + i + 1) * C, :] * scale
            if i < 3:
                gq_ref[:, i * C + g * 128 : i * C + (g + 1) * 128] = block
            else:
                gp_ref[g * 128 : (g + 1) * 128, :] = block.T


def on_device(features, cotangent, hilbert_rank, w_qkv, w_proj):
    shape = jax.ShapeDtypeStruct
    vm = pltpu.VMEM
    dma = pltpu.SemaphoreType.DMA

    def room(span):
        return [
            vm((span[1] // 2, 128), F32), vm((span[1] // 2, 128), F32),
            vm((span[1] // 2, 128), F32), vm((span[2], 128), F32),
        ]

    rows_out, rows_grad, total = pl.pallas_call(
        patch_kernel,
        out_shape=(shape((ROWS, C), BF), shape((ROWS, C), BF), shape((GROWS, 128), F32)),
        in_specs=[VM] * 5,
        out_specs=(VM, VM, ANY),
        scratch_shapes=[
            vm((2, SLOTS, C), BF), vm((2, SLOTS, C), BF), vm((2, SLOTS, C), BF), vm((8, ROWS), F32),
            vm((DEV, 1, 128), F32), vm((DEV, 1, 128), F32), vm((8, SLOTS), F32),
            vm((ROWS, SLOTS), BF), vm((ROWS, 2 * C), BF), vm((ROWS, 2 * C), BF),
            vm((9, ROWS, 128), BF), vm((3, ROWS, 128), BF), vm((C, ROWS), BF), vm((C, ROWS), BF),
            vm((3, ROWS, 128), F32), vm((3, ROWS, 128), F32), vm((C, ROWS), BF), vm((C, ROWS), BF),
            vm((C, ROWS), BF), vm((C, ROWS), BF), vm((3, 3, ROWS, 128), BF), vm((3, ROWS, 128), BF),
            vm((GROWS, 128), F32),
        ] + room(FIRST) + room(SECOND) + [dma((9,)), dma((9,)), dma((10,))],
        compiler_params=pltpu.CompilerParams(
            vmem_limit_bytes=62 * 1024 * 1024, collective_id=0, has_side_effects=True
        ),
        name="patch",
    )(features, cotangent, hilbert_rank.reshape(ROWS // 128, 128), w_qkv, w_proj)
    return pl.pallas_call(
        functools.partial(last_kernel, 1.0 / math.sqrt(ROWS * DEV)),
        out_shape=(
            shape((ROWS, C), BF), shape((ROWS, C), BF), shape((C, 3 * C), F32), shape((C, C), F32),
        ),
        in_specs=[VM] * 3,
        out_specs=(VM,) * 4,
        compiler_params=pltpu.CompilerParams(vmem_limit_bytes=60 * 1024 * 1024),
        name="last",
    )(rows_out, rows_grad, total)


def solution(mesh):
    in_specs = (P(("sx", "sy"), None), P(("sx", "sy"), None), P(("sx", "sy")), P(), P())
    out_specs = (P(("sx", "sy"), None), P(("sx", "sy"), None), P(), P())
    return jax.shard_map(
        on_device, mesh=mesh, in_specs=in_specs, out_specs=out_specs, check_vma=False
    )
```

```python
import functools
import math

import jax
import jax.numpy as jnp
from jax import lax
from jax.experimental import pallas as pl
from jax.experimental.pallas import tpu as pltpu
from jax.sharding import PartitionSpec as P

BF = jnp.bfloat16
F32 = jnp.float32
MESH = pl.DeviceIdType.MESH
HEADS = 24
ROWS = 1024
C = 384
NX = 8
NY = 16
DEV = NX * NY
CHIPS = DEV // 2
CAP = 16
SLOTS = DEV * CAP
RC = 256
HC = 1024
NR = ROWS // RC
SC = NY * CAP
FIRST = (0, 3072, 24)
SECOND = (3072, 2048, 16)
GROWS = FIRST[1] + SECOND[1]
VM = pl.BlockSpec(memory_space=pltpu.VMEM)
ANY = pl.BlockSpec(memory_space=pl.ANY)


def dg(a, b, da, db):
    return lax.dot_general(a, b, (((da,), (db,)), ((), ())), preferred_element_type=F32)


def chunk(i, size):
    return pl.ds(pl.multiple_of(i * size, size), size)


def hot(test):
    return test.astype(F32).astype(BF)


def iota(shape, dim):
    return lax.broadcasted_iota(jnp.int32, shape, dim).astype(F32)


def layer_norm(rows):
    v = rows.astype(F32)
    c = v - jnp.mean(v, axis=1, keepdims=True)
    inv = lax.rsqrt(jnp.mean(c * c, axis=1, keepdims=True) + 1e-5)
    return v, c * inv, inv


def wait_for(ref, sem):
    pltpu.make_async_copy(ref, ref, sem).wait()


class Reduction:
    def __init__(self, span, terms, total, half, own, part, mine, sem, sx, sy):
        self.base, self.count, self.piece = span
        self.terms, self.total = terms, total
        self.half, self.own, self.part, self.mine, self.sem = half, own, part, mine, sem
        self.core = lax.rem(sx, 2)
        self.chip = (sx // 2) * NY + sy
        self.partner = (sx + 1 - 2 * self.core, sy)

    def side(self, core):
        n = self.count // 2
        return pl.ds(pl.multiple_of(self.base + core * n, 8), n)

    def remote(self, src, dst, i, dev):
        return pltpu.make_async_remote_copy(
            src_ref=src, dst_ref=dst, send_sem=self.sem.at[i], recv_sem=self.sem.at[i + 1],
            device_id=dev, device_id_type=MESH,
        )

    def others(self, start):
        def go(d, _):
            t = lax.rem(self.chip + d, CHIPS)
            start(t, ((t // NY) * 2 + self.core, lax.rem(t, NY)))
            return 0

        lax.fori_loop(1, CHIPS, go, 0)

    def placed(self, t):
        n = self.count // 2
        return pl.ds(pl.multiple_of(self.base + self.core * n + t * self.piece, 8), self.piece)

    def pair(self):
        self.remote(self.terms.at[self.side(1 - self.core)], self.half, 0, self.partner).start()

    def scatter(self):
        wait_for(self.half, self.sem.at[1])
        self.own[...] = self.terms[self.side(self.core), :] + self.half[...]
        self.others(
            lambda t, dev: self.remote(
                self.own.at[chunk(t, self.piece)], self.part.at[chunk(self.chip, self.piece)], 2, dev
            ).start()
        )
        self.part[chunk(self.chip, self.piece), :] = self.own[chunk(self.chip, self.piece), :]

    def gather(self):
        rest = self.part.at[pl.ds(0, (CHIPS - 1) * self.piece)]
        wait_for(rest, self.sem.at[3])

        def add(t, acc):
            return acc + self.part[chunk(t, self.piece), :]

        self.mine[...] = lax.fori_loop(0, CHIPS, add, jnp.zeros((self.piece, 128), F32))
        pltpu.make_async_copy(
            self.mine, self.total.at[self.placed(self.chip)], self.sem.at[8]
        ).start()
        self.others(
            lambda t, dev: self.remote(
                self.mine, self.total.at[self.placed(self.chip)], 4, dev
            ).start()
        )

    def give(self):
        rest = self.part.at[pl.ds(0, (CHIPS - 1) * self.piece)]
        wait_for(rest, self.sem.at[5])
        wait_for(self.mine, self.sem.at[8])
        mine = self.total.at[self.side(self.core)]
        self.remote(mine, mine, 6, self.partner).start()

    def finish(self):
        rest = self.part.at[pl.ds(0, (CHIPS - 1) * self.piece)]
        wait_for(self.half, self.sem.at[7])
        wait_for(self.half, self.sem.at[6])
        wait_for(rest, self.sem.at[4])
        wait_for(rest, self.sem.at[2])
        wait_for(self.half, self.sem.at[0])


def patch_kernel(
    x_ref, ct_ref, rank_ref, wqkv_ref, wproj_ref,
    out_ref, gx_ref, total_ref,
    send, got, ret, slot_row, place_out, place_in, place_row, pick, rows, results,
    proj, up, proj_t, up_t, oacc, dqacc, dk_t, dv_t, low_t, ct_t, dproj, att, terms,
    half_a, own_a, part_a, mine_a, half_b, own_b, part_b, mine_b, sem_a, sem_b, sem,
):
    sx = lax.axis_index("sx")
    sy = lax.axis_index("sy")
    me = sx * NY + sy
    barrier = pltpu.get_barrier_semaphore()

    def greet(d, _):
        t = lax.rem(me + d, DEV)
        pl.semaphore_signal(barrier, 1, device_id=(t // NY, lax.rem(t, NY)), device_id_type=MESH)
        return 0

    lax.fori_loop(1, DEV, greet, 0)
    sums = (
        Reduction(FIRST, terms, total_ref, half_a, own_a, part_a, mine_a, sem_a, sx, sy),
        Reduction(SECOND, terms, total_ref, half_b, own_b, part_b, mine_b, sem_b, sx, sy),
    )

    def copy_to(src, dst, t, i):
        pltpu.make_async_remote_copy(
            src_ref=src, dst_ref=dst, send_sem=sem.at[i], recv_sem=sem.at[i + 1],
            device_id=(t // NY, lax.rem(t, NY)), device_id_type=MESH,
        ).start()

    def send_part(part, ref, dst, step, i):
        tx = lax.rem(sx + step, NX)

        def go(d, _):
            t = tx * NY + lax.rem(sy + d, NY)
            copy_to(ref.at[part, chunk(t, CAP)], dst.at[part, chunk(me, CAP)], t, i)
            return 0

        lax.fori_loop(jnp.where(step == 0, 1, 0), NY, go, 0)

    rank = jnp.concatenate([rank_ref[i : i + 1, :] for i in range(ROWS // 128)], axis=1)
    owner = rank // ROWS
    place = rank - owner * ROWS
    owned = iota((DEV, ROWS), 0) == owner.astype(F32)
    before = iota((ROWS, ROWS), 0) < iota((ROWS, ROWS), 1)
    counts = jnp.dot(hot(owned), hot(before), preferred_element_type=F32)
    earlier = jnp.sum(jnp.where(owned, counts, 0.0), axis=0, keepdims=True)
    slot = owner.astype(F32) * CAP + earlier
    slot_row[...] = jnp.broadcast_to(slot, slot_row.shape)
    high = place // 32
    line = iota((128, ROWS), 0) == earlier
    codes = [
        dg(hot(owned), jnp.where(line, v.astype(F32), 0.0).astype(BF), 1, 1)
        for v in (high + 1, place - high * 32)
    ]
    place_out[...] = (codes[0] * 32.0 + codes[1]).reshape(DEV, 1, 128)
    pl.semaphore_wait(barrier, DEV - 1)

    def packs(part, src):
        def step(k, _):
            tx = lax.rem(sx + k, NX)
            ids = iota((SC, ROWS), 0) + (tx * SC).astype(F32)
            send[part, chunk(tx, SC), :] = jnp.dot(
                hot(ids == slot), src[...], preferred_element_type=F32
            ).astype(BF)

            @pl.when(k > 0)
            def _():
                send_part(part, send, got, k - 1, 2 * part)

            return 0

        lax.fori_loop(0, NX, step, 0)

    packs(0, x_ref)

    def send_place(d, _):
        t = lax.rem(me + d, DEV)
        copy_to(place_out.at[t], place_in.at[me], t, 4)
        return 0

    lax.fori_loop(1, DEV, send_place, 0)
    place_in[me] = place_out[me]
    send_part(0, send, got, NX - 1, 0)
    packs(1, ct_ref)
    send_part(1, send, got, NX - 1, 2)
    mine = chunk(me, CAP)
    got[0, mine, :] = send[0, mine, :]
    got[1, mine, :] = send[1, mine, :]

    wait_for(place_in.at[pl.ds(0, DEV - 1)], sem.at[5])
    code = place_in[...].reshape(DEV, 128).T[0:CAP, :]
    big = jnp.floor(code * (1.0 / 32.0))
    spread = hot(iota((DEV, SLOTS), 0) == jnp.floor(iota((DEV, SLOTS), 1) * (1.0 / CAP)))
    both = [
        jnp.dot(v.astype(BF), spread, preferred_element_type=F32)
        for v in (big, code - big * 32.0)
    ]
    lanes = iota((CAP, SLOTS), 1)
    keep = (lanes - jnp.floor(lanes * (1.0 / CAP)) * CAP) == iota((CAP, SLOTS), 0)
    found = jnp.sum(jnp.where(keep, both[0] * 32.0 + both[1], 0.0), axis=0, keepdims=True)
    place_row[...] = jnp.broadcast_to(found - 32.0, place_row.shape)

    wait_for(got.at[0, pl.ds(0, SLOTS - CAP)], sem.at[1])

    def forward_rows(r, _):
        rs = chunk(r, RC)
        ids = iota((RC, SLOTS), 0) + (r * RC).astype(F32)
        q = hot(ids == place_row[0:1, :])
        pick[rs, :] = q
        x = jnp.dot(q, got[0], preferred_element_type=F32).astype(BF)
        rows[rs, :C] = x
        _, n, _ = layer_norm(x)
        nl = n.astype(BF)
        low_t[:, rs] = nl.T
        p = jnp.dot(nl, wqkv_ref[...], preferred_element_type=F32).astype(BF)
        for g in range(9):
            blk = p[:, g * 128 : (g + 1) * 128]
            proj[g, rs, :] = blk
            if g < 3:
                proj_t[g * 128 : (g + 1) * 128, rs] = (blk * BF(0.25)).T
        return 0

    lax.fori_loop(0, NR, forward_rows, 0)
    oacc[...] = jnp.zeros_like(oacc)
    dqacc[...] = jnp.zeros_like(dqacc)
    terms[GROWS - SECOND[1] + 4 * C :, :] = jnp.zeros((SECOND[1] - 4 * C, 128), F32)
    wait_for(got.at[1, pl.ds(0, SLOTS - CAP)], sem.at[3])

    def upstream_rows(r, _):
        rs = chunk(r, RC)
        ct = jnp.dot(pick[rs, :], got[1], preferred_element_type=F32).astype(BF)
        rows[rs, C:] = ct
        ct_t[:, rs] = ct.T
        u = dg(ct, wproj_ref[...], 1, 1).astype(BF)
        for g in range(3):
            blk = u[:, g * 128 : (g + 1) * 128]
            up[g, rs, :] = blk
            up_t[g * 128 : (g + 1) * 128, rs] = blk.T
        return 0

    lax.fori_loop(0, NR, upstream_rows, 0)
    lane = lax.broadcasted_iota(jnp.int32, (1, 128), 1) // 16

    def head(h, _):
        g = h // 8
        mask = hot(lane == (h - g * 8))
        k = proj[3 + g]
        v = proj[6 + g]
        km = k * (mask * BF(0.25))
        vm = v * mask
        hs = chunk(h, 16)
        dk = jnp.zeros((16, ROWS), F32)
        dv = jnp.zeros((16, ROWS), F32)
        for r in range(ROWS // HC):
            rs = slice(r * HC, (r + 1) * HC)
            qm = proj[g, rs, :] * (mask * BF(0.25))
            um = up[g, rs, :] * mask
            s = dg(qm, k, 1, 1)
            dp = dg(um, v, 1, 1)
            e = jnp.exp(s - jnp.max(s, axis=1, keepdims=True))
            linv = 1.0 / jnp.sum(e, axis=1, keepdims=True)
            mid = jnp.sum(e * dp, axis=1, keepdims=True) * linv
            p = e * linv
            pb = p.astype(BF)
            ds = (p * (dp - mid)).astype(BF)
            oacc[g, rs, :] += jnp.dot(pb, vm, preferred_element_type=F32)
            dqacc[g, rs, :] += jnp.dot(ds, km, preferred_element_type=F32)
            dk = dk + jnp.dot(proj_t[hs, rs], ds, preferred_element_type=F32)
            dv = dv + jnp.dot(up_t[hs, rs], pb, preferred_element_type=F32)
        dk_t[hs, :] = dk.astype(BF)
        dv_t[hs, :] = dv.astype(BF)

        @pl.when(h == 16)
        def _():
            sums[0].scatter()

        @pl.when(h == 21)
        def _():
            sums[0].gather()

        @pl.when(h - g * 8 == 7)
        def _():
            gs = chunk(g, 128)
            base = g * (4 * C)
            parts = (
                dqacc[g].astype(BF),
                dk_t[gs, :].T,
                dv_t[gs, :].T,
                oacc[g].astype(BF),
            )
            for i, part in enumerate(parts):
                if i < 3:
                    dproj[i, g] = part
                else:
                    att[g] = part
                terms[pl.ds(pl.multiple_of(base + i * C, 128), C), :] = jnp.dot(
                    (ct_t if i == 3 else low_t)[...], part, preferred_element_type=F32
                )

        @pl.when(h == 15)
        def _():
            sums[0].pair()

        return 0

    lax.fori_loop(0, HEADS, head, 0)
    sums[1].pair()

    def epilogue(r, _):
        @pl.when(r == 1)
        def _():
            sums[1].scatter()

        rs = chunk(r, RC)
        v, n, inv = layer_norm(rows[rs, :C])
        a = jnp.concatenate([att[g, rs, :] for g in range(3)], axis=1)
        dpj = jnp.concatenate([dproj[i, g, rs, :] for i in range(3) for g in range(3)], axis=1)
        ct = rows[rs, C:]
        results[rs, :C] = (v + jnp.dot(a, wproj_ref[...], preferred_element_type=F32)).astype(BF)
        dn = dg(dpj, wqkv_ref[...], 1, 1)
        dm = jnp.mean(dn, axis=1, keepdims=True)
        cm = jnp.mean(dn * n, axis=1, keepdims=True)
        results[rs, C:] = (ct.astype(F32) + inv * (dn - dm - n * cm)).astype(BF)
        return 0

    lax.fori_loop(0, NR, epilogue, 0)
    sums[0].give()
    sums[1].gather()
    for part in range(2):
        wait_for(send.at[part, pl.ds(0, SLOTS - CAP)], sem.at[2 * part])

    def backs(part):
        def step(k, _):
            tx = lax.rem(sx + k, NX)
            ss = chunk(tx, SC)
            spot = jnp.broadcast_to(place_row[0:1, ss], (128, SC)).T[:, 0:1]
            q = hot(iota((SC, ROWS), 1) == spot)
            send[part, ss, :] = jnp.dot(
                q, results[:, part * C : (part + 1) * C], preferred_element_type=F32
            ).astype(BF)

            @pl.when(k > 0)
            def _():
                send_part(part, send, ret, k - 1, 6 + 2 * part)

            return 0

        lax.fori_loop(0, NX, step, 0)
        send_part(part, send, ret, NX - 1, 6 + 2 * part)
        ret[part, mine, :] = send[part, mine, :]

    backs(0)
    backs(1)

    def takes(r, _):
        rs = chunk(r, RC)
        spot = jnp.broadcast_to(slot_row[0:1, rs], (128, RC)).T[:, 0:1]
        pick[rs, :] = hot(iota((RC, SLOTS), 1) == spot)
        return 0

    lax.fori_loop(0, NR, takes, 0)
    sums[1].give()
    for part, dst in enumerate((out_ref, gx_ref)):
        wait_for(ret.at[part, pl.ds(0, SLOTS - CAP)], sem.at[7 + 2 * part])

        def unpack(r, _, part=part, dst=dst):
            rs = chunk(r, RC)
            dst[rs, :] = jnp.dot(pick[rs, :], ret[part], preferred_element_type=F32).astype(BF)
            return 0

        lax.fori_loop(0, NR, unpack, 0)
    wait_for(place_out.at[pl.ds(0, DEV - 1)], sem.at[4])
    for part in range(2):
        wait_for(send.at[part, pl.ds(0, SLOTS - CAP)], sem.at[6 + 2 * part])
    sums[0].finish()
    sums[1].finish()


def last_kernel(scale, x_ref, g_ref, total_ref, out_ref, gx_ref, gq_ref, gp_ref):
    out_ref[...] = x_ref[...]
    gx_ref[...] = g_ref[...]
    for g in range(3):
        for i in range(4):
            block = total_ref[(4 * g + i) * C : (4 * g + i + 1) * C, :] * scale
            if i < 3:
                gq_ref[:, i * C + g * 128 : i * C + (g + 1) * 128] = block
            else:
                gp_ref[g * 128 : (g + 1) * 128, :] = block.T


def on_device(features, cotangent, hilbert_rank, w_qkv, w_proj):
    shape = jax.ShapeDtypeStruct
    vm = pltpu.VMEM
    dma = pltpu.SemaphoreType.DMA

    def room(span):
        return [
            vm((span[1] // 2, 128), F32), vm((span[1] // 2, 128), F32),
            vm((span[1] // 2, 128), F32), vm((span[2], 128), F32),
        ]

    rows_out, rows_grad, total = pl.pallas_call(
        patch_kernel,
        out_shape=(shape((ROWS, C), BF), shape((ROWS, C), BF), shape((GROWS, 128), F32)),
        in_specs=[VM] * 5,
        out_specs=(VM, VM, ANY),
        scratch_shapes=[
            vm((2, SLOTS, C), BF), vm((2, SLOTS, C), BF), vm((2, SLOTS, C), BF), vm((8, ROWS), F32),
            vm((DEV, 1, 128), F32), vm((DEV, 1, 128), F32), vm((8, SLOTS), F32),
            vm((ROWS, SLOTS), BF), vm((ROWS, 2 * C), BF), vm((ROWS, 2 * C), BF),
            vm((9, ROWS, 128), BF), vm((3, ROWS, 128), BF), vm((C, ROWS), BF), vm((C, ROWS), BF),
            vm((3, ROWS, 128), F32), vm((3, ROWS, 128), F32), vm((C, ROWS), BF), vm((C, ROWS), BF),
            vm((C, ROWS), BF), vm((C, ROWS), BF), vm((3, 3, ROWS, 128), BF), vm((3, ROWS, 128), BF),
            vm((GROWS, 128), F32),
        ] + room(FIRST) + room(SECOND) + [dma((9,)), dma((9,)), dma((10,))],
        compiler_params=pltpu.CompilerParams(
            vmem_limit_bytes=62 * 1024 * 1024, collective_id=0, has_side_effects=True
        ),
        name="patch",
    )(features, cotangent, hilbert_rank.reshape(ROWS // 128, 128), w_qkv, w_proj)
    return pl.pallas_call(
        functools.partial(last_kernel, 1.0 / math.sqrt(ROWS * DEV)),
        out_shape=(
            shape((ROWS, C), BF), shape((ROWS, C), BF), shape((C, 3 * C), F32), shape((C, C), F32),
        ),
        in_specs=[VM] * 3,
        out_specs=(VM,) * 4,
        compiler_params=pltpu.CompilerParams(vmem_limit_bytes=60 * 1024 * 1024),
        name="last",
    )(rows_out, rows_grad, total)


def solution(mesh):
    in_specs = (P(("sx", "sy"), None), P(("sx", "sy"), None), P(("sx", "sy")), P(), P())
    out_specs = (P(("sx", "sy"), None), P(("sx", "sy"), None), P(), P())
    return jax.shard_map(
        on_device, mesh=mesh, in_specs=in_specs, out_specs=out_specs, check_vma=False
    )
```

```python
import functools
import math

import jax
import jax.numpy as jnp
from jax import lax
from jax.experimental import pallas as pl
from jax.experimental.pallas import tpu as pltpu
from jax.sharding import PartitionSpec as P

BF = jnp.bfloat16
F32 = jnp.float32
MESH = pl.DeviceIdType.MESH
HEADS = 24
ROWS = 1024
C = 384
NX = 8
NY = 16
DEV = NX * NY
CHIPS = DEV // 2
CAP = 16
SLOTS = DEV * CAP
RC = 256
HC = 1024
NR = ROWS // RC
SC = NY * CAP
FIRST = (0, 3072, 24)
SECOND = (3072, 2048, 16)
GROWS = FIRST[1] + SECOND[1]
VM = pl.BlockSpec(memory_space=pltpu.VMEM)
ANY = pl.BlockSpec(memory_space=pl.ANY)


def dg(a, b, da, db):
    return lax.dot_general(a, b, (((da,), (db,)), ((), ())), preferred_element_type=F32)


def chunk(i, size):
    return pl.ds(pl.multiple_of(i * size, size), size)


def hot(test):
    return test.astype(F32).astype(BF)


def iota(shape, dim):
    return lax.broadcasted_iota(jnp.int32, shape, dim).astype(F32)


def layer_norm(rows):
    v = rows.astype(F32)
    c = v - jnp.mean(v, axis=1, keepdims=True)
    inv = lax.rsqrt(jnp.mean(c * c, axis=1, keepdims=True) + 1e-5)
    return v, c * inv, inv


def wait_for(ref, sem):
    pltpu.make_async_copy(ref, ref, sem).wait()


class Reduction:
    def __init__(self, span, terms, total, half, own, part, mine, sem, sx, sy):
        self.base, self.count, self.piece = span
        self.terms, self.total = terms, total
        self.half, self.own, self.part, self.mine, self.sem = half, own, part, mine, sem
        self.core = lax.rem(sx, 2)
        self.chip = (sx // 2) * NY + sy
        self.partner = (sx + 1 - 2 * self.core, sy)

    def side(self, core):
        n = self.count // 2
        return pl.ds(pl.multiple_of(self.base + core * n, 8), n)

    def remote(self, src, dst, i, dev):
        return pltpu.make_async_remote_copy(
            src_ref=src, dst_ref=dst, send_sem=self.sem.at[i], recv_sem=self.sem.at[i + 1],
            device_id=dev, device_id_type=MESH,
        )

    def others(self, start):
        def go(d, _):
            t = lax.rem(self.chip + d, CHIPS)
            start(t, ((t // NY) * 2 + self.core, lax.rem(t, NY)))
            return 0

        lax.fori_loop(1, CHIPS, go, 0)

    def placed(self, t):
        n = self.count // 2
        return pl.ds(pl.multiple_of(self.base + self.core * n + t * self.piece, 8), self.piece)

    def pair(self):
        self.remote(self.terms.at[self.side(1 - self.core)], self.half, 0, self.partner).start()

    def scatter(self):
        wait_for(self.half, self.sem.at[1])
        self.own[...] = self.terms[self.side(self.core), :] + self.half[...]
        self.others(
            lambda t, dev: self.remote(
                self.own.at[chunk(t, self.piece)], self.part.at[chunk(self.chip, self.piece)], 2, dev
            ).start()
        )
        self.part[chunk(self.chip, self.piece), :] = self.own[chunk(self.chip, self.piece), :]

    def gather(self):
        rest = self.part.at[pl.ds(0, (CHIPS - 1) * self.piece)]
        wait_for(rest, self.sem.at[3])

        def add(t, acc):
            return acc + self.part[chunk(t, self.piece), :]

        self.mine[...] = lax.fori_loop(0, CHIPS, add, jnp.zeros((self.piece, 128), F32))
        pltpu.make_async_copy(
            self.mine, self.total.at[self.placed(self.chip)], self.sem.at[8]
        ).start()
        self.others(
            lambda t, dev: self.remote(
                self.mine, self.total.at[self.placed(self.chip)], 4, dev
            ).start()
        )

    def give(self):
        rest = self.part.at[pl.ds(0, (CHIPS - 1) * self.piece)]
        wait_for(rest, self.sem.at[5])
        wait_for(self.mine, self.sem.at[8])
        mine = self.total.at[self.side(self.core)]
        self.remote(mine, mine, 6, self.partner).start()

    def finish(self):
        rest = self.part.at[pl.ds(0, (CHIPS - 1) * self.piece)]
        wait_for(self.half, self.sem.at[7])
        wait_for(self.half, self.sem.at[6])
        wait_for(rest, self.sem.at[4])
        wait_for(rest, self.sem.at[2])
        wait_for(self.half, self.sem.at[0])


def patch_kernel(
    x_ref, ct_ref, rank_ref, wqkv_ref, wproj_ref,
    out_ref, gx_ref, total_ref,
    send, got, ret, slot_row, place_out, place_in, place_row, pick, rows, results,
    proj, up, proj_t, up_t, oacc, dqacc, dk_t, dv_t, low_t, ct_t, dproj, att, terms,
    half_a, own_a, part_a, mine_a, half_b, own_b, part_b, mine_b, sem_a, sem_b, sem,
):
    sx = lax.axis_index("sx")
    sy = lax.axis_index("sy")
    me = sx * NY + sy
    barrier = pltpu.get_barrier_semaphore()

    def greet(d, _):
        t = lax.rem(me + d, DEV)
        pl.semaphore_signal(barrier, 1, device_id=(t // NY, lax.rem(t, NY)), device_id_type=MESH)
        return 0

    lax.fori_loop(1, DEV, greet, 0)
    sums = (
        Reduction(FIRST, terms, total_ref, half_a, own_a, part_a, mine_a, sem_a, sx, sy),
        Reduction(SECOND, terms, total_ref, half_b, own_b, part_b, mine_b, sem_b, sx, sy),
    )

    def copy_to(src, dst, t, i):
        pltpu.make_async_remote_copy(
            src_ref=src, dst_ref=dst, send_sem=sem.at[i], recv_sem=sem.at[i + 1],
            device_id=(t // NY, lax.rem(t, NY)), device_id_type=MESH,
        ).start()

    def send_part(part, ref, dst, step, i):
        tx = lax.rem(sx + step, NX)

        def go(d, _):
            t = tx * NY + lax.rem(sy + d, NY)
            copy_to(ref.at[part, chunk(t, CAP)], dst.at[part, chunk(me, CAP)], t, i)
            return 0

        lax.fori_loop(jnp.where(step == 0, 1, 0), NY, go, 0)

    rank = jnp.concatenate([rank_ref[i : i + 1, :] for i in range(ROWS // 128)], axis=1)
    owner = rank // ROWS
    place = rank - owner * ROWS
    owned = iota((DEV, ROWS), 0) == owner.astype(F32)
    before = iota((ROWS, ROWS), 0) < iota((ROWS, ROWS), 1)
    counts = jnp.dot(hot(owned), hot(before), preferred_element_type=F32)
    earlier = jnp.sum(jnp.where(owned, counts, 0.0), axis=0, keepdims=True)
    slot = owner.astype(F32) * CAP + earlier
    slot_row[...] = jnp.broadcast_to(slot, slot_row.shape)
    high = place // 32
    line = iota((128, ROWS), 0) == earlier
    codes = [
        dg(hot(owned), jnp.where(line, v.astype(F32), 0.0).astype(BF), 1, 1)
        for v in (high + 1, place - high * 32)
    ]
    place_out[...] = (codes[0] * 32.0 + codes[1]).reshape(DEV, 1, 128)
    pl.semaphore_wait(barrier, DEV - 1)

    def packs(part, src):
        def step(k, _):
            tx = lax.rem(sx + k, NX)
            ids = iota((SC, ROWS), 0) + (tx * SC).astype(F32)
            send[part, chunk(tx, SC), :] = jnp.dot(
                hot(ids == slot), src[...], preferred_element_type=F32
            ).astype(BF)

            @pl.when(k > 0)
            def _():
                send_part(part, send, got, k - 1, 2 * part)

            return 0

        lax.fori_loop(0, NX, step, 0)

    packs(0, x_ref)

    def send_place(d, _):
        t = lax.rem(me + d, DEV)
        copy_to(place_out.at[t], place_in.at[me], t, 4)
        return 0

    lax.fori_loop(1, DEV, send_place, 0)
    place_in[me] = place_out[me]
    send_part(0, send, got, NX - 1, 0)
    packs(1, ct_ref)
    send_part(1, send, got, NX - 1, 2)
    mine = chunk(me, CAP)
    got[0, mine, :] = send[0, mine, :]
    got[1, mine, :] = send[1, mine, :]

    wait_for(place_in.at[pl.ds(0, DEV - 1)], sem.at[5])
    code = place_in[...].reshape(DEV, 128).T[0:CAP, :]
    big = jnp.floor(code * (1.0 / 32.0))
    spread = hot(iota((DEV, SLOTS), 0) == jnp.floor(iota((DEV, SLOTS), 1) * (1.0 / CAP)))
    both = [
        jnp.dot(v.astype(BF), spread, preferred_element_type=F32)
        for v in (big, code - big * 32.0)
    ]
    lanes = iota((CAP, SLOTS), 1)
    keep = (lanes - jnp.floor(lanes * (1.0 / CAP)) * CAP) == iota((CAP, SLOTS), 0)
    found = jnp.sum(jnp.where(keep, both[0] * 32.0 + both[1], 0.0), axis=0, keepdims=True)
    place_row[...] = jnp.broadcast_to(found - 32.0, place_row.shape)

    wait_for(got.at[0, pl.ds(0, SLOTS - CAP)], sem.at[1])

    def forward_rows(r, _):
        rs = chunk(r, RC)
        ids = iota((RC, SLOTS), 0) + (r * RC).astype(F32)
        q = hot(ids == place_row[0:1, :])
        pick[rs, :] = q
        x = jnp.dot(q, got[0], preferred_element_type=F32).astype(BF)
        rows[rs, :C] = x
        _, n, _ = layer_norm(x)
        nl = n.astype(BF)
        low_t[:, rs] = nl.T
        p = jnp.dot(nl, wqkv_ref[...], preferred_element_type=F32).astype(BF)
        for g in range(9):
            blk = p[:, g * 128 : (g + 1) * 128]
            proj[g, rs, :] = blk
            if g < 3:
                proj_t[g * 128 : (g + 1) * 128, rs] = (blk * BF(0.25)).T
        return 0

    lax.fori_loop(0, NR, forward_rows, 0)
    oacc[...] = jnp.zeros_like(oacc)
    dqacc[...] = jnp.zeros_like(dqacc)
    terms[GROWS - SECOND[1] + 4 * C :, :] = jnp.zeros((SECOND[1] - 4 * C, 128), F32)
    wait_for(got.at[1, pl.ds(0, SLOTS - CAP)], sem.at[3])

    def upstream_rows(r, _):
        rs = chunk(r, RC)
        ct = jnp.dot(pick[rs, :], got[1], preferred_element_type=F32).astype(BF)
        rows[rs, C:] = ct
        ct_t[:, rs] = ct.T
        u = dg(ct, wproj_ref[...], 1, 1).astype(BF)
        for g in range(3):
            blk = u[:, g * 128 : (g + 1) * 128]
            up[g, rs, :] = blk
            up_t[g * 128 : (g + 1) * 128, rs] = blk.T
        return 0

    lax.fori_loop(0, NR, upstream_rows, 0)
    lane = lax.broadcasted_iota(jnp.int32, (1, 128), 1) // 16

    def head(h, _):
        g = h // 8
        mask = hot(lane == (h - g * 8))
        k = proj[3 + g]
        v = proj[6 + g]
        km = k * (mask * BF(0.25))
        vm = v * mask
        hs = chunk(h, 16)
        dk = jnp.zeros((16, ROWS), F32)
        dv = jnp.zeros((16, ROWS), F32)
        for r in range(ROWS // HC):
            rs = slice(r * HC, (r + 1) * HC)
            qm = proj[g, rs, :] * (mask * BF(0.25))
            um = up[g, rs, :] * mask
            s = dg(qm, k, 1, 1)
            dp = dg(um, v, 1, 1)
            e = jnp.exp(s - jnp.max(s, axis=1, keepdims=True))
            linv = 1.0 / jnp.sum(e, axis=1, keepdims=True)
            mid = jnp.sum(e * dp, axis=1, keepdims=True) * linv
            p = e * linv
            pb = p.astype(BF)
            ds = (p * (dp - mid)).astype(BF)
            oacc[g, rs, :] += jnp.dot(pb, vm, preferred_element_type=F32)
            dqacc[g, rs, :] += jnp.dot(ds, km, preferred_element_type=F32)
            dk = dk + jnp.dot(proj_t[hs, rs], ds, preferred_element_type=F32)
            dv = dv + jnp.dot(up_t[hs, rs], pb, preferred_element_type=F32)
        dk_t[hs, :] = dk.astype(BF)
        dv_t[hs, :] = dv.astype(BF)

        @pl.when(h == 16)
        def _():
            sums[0].scatter()

        @pl.when(h == 21)
        def _():
            sums[0].gather()

        @pl.when(h - g * 8 == 7)
        def _():
            gs = chunk(g, 128)
            base = g * (4 * C)
            parts = (
                dqacc[g].astype(BF),
                dk_t[gs, :].T,
                dv_t[gs, :].T,
                oacc[g].astype(BF),
            )
            for i, part in enumerate(parts):
                if i < 3:
                    dproj[i, g] = part
                else:
                    att[g] = part
                terms[pl.ds(pl.multiple_of(base + i * C, 128), C), :] = jnp.dot(
                    (ct_t if i == 3 else low_t)[...], part, preferred_element_type=F32
                )

        @pl.when(h == 15)
        def _():
            sums[0].pair()

        return 0

    lax.fori_loop(0, HEADS, head, 0)
    sums[1].pair()

    def epilogue(r, _):
        @pl.when(r == 1)
        def _():
            sums[1].scatter()

        rs = chunk(r, RC)
        v, n, inv = layer_norm(rows[rs, :C])
        a = jnp.concatenate([att[g, rs, :] for g in range(3)], axis=1)
        dpj = jnp.concatenate([dproj[i, g, rs, :] for i in range(3) for g in range(3)], axis=1)
        ct = rows[rs, C:]
        results[rs, :C] = (v + jnp.dot(a, wproj_ref[...], preferred_element_type=F32)).astype(BF)
        dn = dg(dpj, wqkv_ref[...], 1, 1)
        dm = jnp.mean(dn, axis=1, keepdims=True)
        cm = jnp.mean(dn * n, axis=1, keepdims=True)
        results[rs, C:] = (ct.astype(F32) + inv * (dn - dm - n * cm)).astype(BF)
        return 0

    lax.fori_loop(0, NR, epilogue, 0)
    sums[0].give()
    for part in range(2):
        wait_for(send.at[part, pl.ds(0, SLOTS - CAP)], sem.at[2 * part])

    def backs(part):
        def step(k, _):
            tx = lax.rem(sx + k, NX)
            ss = chunk(tx, SC)
            spot = jnp.broadcast_to(place_row[0:1, ss], (128, SC)).T[:, 0:1]
            q = hot(iota((SC, ROWS), 1) == spot)
            send[part, ss, :] = jnp.dot(
                q, results[:, part * C : (part + 1) * C], preferred_element_type=F32
            ).astype(BF)

            @pl.when(k > 0)
            def _():
                send_part(part, send, ret, k - 1, 6 + 2 * part)

            return 0

        lax.fori_loop(0, NX, step, 0)
        send_part(part, send, ret, NX - 1, 6 + 2 * part)
        ret[part, mine, :] = send[part, mine, :]

    backs(0)
    sums[1].gather()
    backs(1)

    def takes(r, _):
        rs = chunk(r, RC)
        spot = jnp.broadcast_to(slot_row[0:1, rs], (128, RC)).T[:, 0:1]
        pick[rs, :] = hot(iota((RC, SLOTS), 1) == spot)
        return 0

    lax.fori_loop(0, NR, takes, 0)
    for part, dst in enumerate((out_ref, gx_ref)):
        wait_for(ret.at[part, pl.ds(0, SLOTS - CAP)], sem.at[7 + 2 * part])

        def unpack(r, _, part=part, dst=dst):
            rs = chunk(r, RC)
            dst[rs, :] = jnp.dot(pick[rs, :], ret[part], preferred_element_type=F32).astype(BF)
            return 0

        lax.fori_loop(0, NR, unpack, 0)
        if part == 0:
            sums[1].give()
    wait_for(place_out.at[pl.ds(0, DEV - 1)], sem.at[4])
    for part in range(2):
        wait_for(send.at[part, pl.ds(0, SLOTS - CAP)], sem.at[6 + 2 * part])
    sums[0].finish()
    sums[1].finish()


def last_kernel(scale, x_ref, g_ref, total_ref, out_ref, gx_ref, gq_ref, gp_ref):
    out_ref[...] = x_ref[...]
    gx_ref[...] = g_ref[...]
    for g in range(3):
        for i in range(4):
            block = total_ref[(4 * g + i) * C : (4 * g + i + 1) * C, :] * scale
            if i < 3:
                gq_ref[:, i * C + g * 128 : i * C + (g + 1) * 128] = block
            else:
                gp_ref[g * 128 : (g + 1) * 128, :] = block.T


def on_device(features, cotangent, hilbert_rank, w_qkv, w_proj):
    shape = jax.ShapeDtypeStruct
    vm = pltpu.VMEM
    dma = pltpu.SemaphoreType.DMA

    def room(span):
        return [
            vm((span[1] // 2, 128), F32), vm((span[1] // 2, 128), F32),
            vm((span[1] // 2, 128), F32), vm((span[2], 128), F32),
        ]

    rows_out, rows_grad, total = pl.pallas_call(
        patch_kernel,
        out_shape=(shape((ROWS, C), BF), shape((ROWS, C), BF), shape((GROWS, 128), F32)),
        in_specs=[VM] * 5,
        out_specs=(VM, VM, ANY),
        scratch_shapes=[
            vm((2, SLOTS, C), BF), vm((2, SLOTS, C), BF), vm((2, SLOTS, C), BF), vm((8, ROWS), F32),
            vm((DEV, 1, 128), F32), vm((DEV, 1, 128), F32), vm((8, SLOTS), F32),
            vm((ROWS, SLOTS), BF), vm((ROWS, 2 * C), BF), vm((ROWS, 2 * C), BF),
            vm((9, ROWS, 128), BF), vm((3, ROWS, 128), BF), vm((C, ROWS), BF), vm((C, ROWS), BF),
            vm((3, ROWS, 128), F32), vm((3, ROWS, 128), F32), vm((C, ROWS), BF), vm((C, ROWS), BF),
            vm((C, ROWS), BF), vm((C, ROWS), BF), vm((3, 3, ROWS, 128), BF), vm((3, ROWS, 128), BF),
            vm((GROWS, 128), F32),
        ] + room(FIRST) + room(SECOND) + [dma((9,)), dma((9,)), dma((10,))],
        compiler_params=pltpu.CompilerParams(
            vmem_limit_bytes=62 * 1024 * 1024, collective_id=0, has_side_effects=True
        ),
        name="patch",
    )(features, cotangent, hilbert_rank.reshape(ROWS // 128, 128), w_qkv, w_proj)
    return pl.pallas_call(
        functools.partial(last_kernel, 1.0 / math.sqrt(ROWS * DEV)),
        out_shape=(
            shape((ROWS, C), BF), shape((ROWS, C), BF), shape((C, 3 * C), F32), shape((C, C), F32),
        ),
        in_specs=[VM] * 3,
        out_specs=(VM,) * 4,
        compiler_params=pltpu.CompilerParams(vmem_limit_bytes=60 * 1024 * 1024),
        name="last",
    )(rows_out, rows_grad, total)


def solution(mesh):
    in_specs = (P(("sx", "sy"), None), P(("sx", "sy"), None), P(("sx", "sy")), P(), P())
    out_specs = (P(("sx", "sy"), None), P(("sx", "sy"), None), P(), P())
    return jax.shard_map(
        on_device, mesh=mesh, in_specs=in_specs, out_specs=out_specs, check_vma=False
    )
```
